256 devices in a mesh: seq: 32 (over y_lo, z, core), tp: 8 (over x, y_hi).
Axes of the slice: x: 4, y: 4 (y_hi: 2, y_lo: 2; y = y_hi * 2 + y_lo), z: 8, core: 2. Of those that a mesh axis runs over, the one named last changes fastest.
Arguments:
- hidden_in: bfloat16 [4, 2048, 4096], P(None, 'seq'), may hold values from -6 to 6
- ln_gain: float32 [4096], replicated, may hold values from 0.1 to 1.9
- ln_bias: float32 [4096], replicated, may hold values from -3 to 3
- w_qkv: bfloat16 [3, 4096, 4096], P(None, 'seq', 'tp'), may hold values from -0.09375 to 0.09375
- w_out: bfloat16 [4096, 4096], P('tp', 'seq'), may hold values from -1.5 to 1.5
- cache_kv: bfloat16 [4, 512, 2, 4096], P(None, 'seq', None, 'tp'), may hold values from -500 to 500
- cache_len: int32 [4], replicated, may hold values from 128 to 512, as said below
- owner: int32 [8192, 1], P('seq'), may hold values from 0 to 31; in each aligned block of 256 rows (0 to 255, 256 to 511, ...) at most 8 rows name the same one
Outputs:
- attn_out: bfloat16 [4, 2048, 4096], P(None, 'seq', 'tp')
- appended: bfloat16 [8192, 2, 4096], P('seq', None, 'tp')
The draws below stay inside these ranges and needn't reach their ends.
Inputs may be any that keep to these rules, and one draw needn't show every extreme that they name: `cache_len`: at least 128; one request's cache holds exactly 512 positions. Among the 256 tokens of one device no owner is named more than 8 times.
All inputs are finite; a program needn't handle non-finite values.
Results may differ from the reference program's by a relative error of at most 0.013.
The reference program's roundings to bfloat16 on the way count: a program that leaves them out, or rounds other values in their place, can miss the bound.
Values may be sent and summed in bfloat16 or wider, within the bound.
A program may use at most 128 MiB of HBM per device.

```python
import math
import jax
import jax.numpy as jnp
import numpy as np
from jax import lax

D = 4096
HEADS = 16
HD = 256
ROT = 64
REQ = 4
SLOTS = 8
TOK_DEV = 256
TOKENS = 8192
NEW_LEN = 2048
CACHE = 512
N_SEQ = 32
N_TP = 8


def draw_cache_kv(key, part):
    columns = HEADS * HD
    shape_all = (REQ, CACHE, 2, columns)
    base = jnp.clip(jax.random.normal(jax.random.fold_in(key, 11), shape_all, jnp.float32), -6.0, 6.0)
    return base.astype(jnp.bfloat16)


def draw_cache_len(key, part):
    lengths = jax.random.randint(jax.random.fold_in(key, 21), (REQ,), CACHE // 4, CACHE + 1)
    chosen = jax.random.randint(jax.random.fold_in(key, 22), (), 0, REQ)
    return jnp.where(jnp.arange(REQ) == chosen, CACHE, lengths).astype(jnp.int32)


def steps_of(stream_key, dims, split, low, largest):
    loudness, own = 1.0, jax.random.fold_in(stream_key, 6)
    for dim, parts in split:
        draws = jnp.exp(jax.random.uniform(jax.random.fold_in(own, dim), (parts,), jnp.float32, low / len(split), largest / len(split)))
        loudness = loudness * jnp.repeat(draws, dims[dim] // parts).reshape([-1 if axis == dim else 1 for axis in range(len(dims))])
    return loudness


def assign_block(key, own, number, rows, amount, top, bound, lean):
    ranking = jax.random.permutation(key, amount)
    packed, usual = shares(amount, rows * top, bound, lean, True), shares(amount, rows * top, bound, lean, False)
    places = jnp.arange(amount)

    def named(sizes, rotation):
        used = int((sizes > 0).sum())
        fixed = max(1, used // 4)
        moved = fixed + (places - fixed + rotation * (used - fixed)) % max(1, amount - fixed)
        return jnp.zeros((amount,), jnp.int32).at[ranking[jnp.where(places < fixed, places, moved)]].set(jnp.asarray(sizes, jnp.int32))

    sizes = jnp.where(number % 4 == 0, named(packed, number // 4), named(usual, number - number // 4 - 1))
    mixed = jax.random.permutation(jax.random.fold_in(own, 3), amount)
    giver, taker = mixed[0:amount // 2 * 2:2], mixed[1:amount // 2 * 2:2]
    room = jnp.minimum(sizes[giver] - 1, bound - sizes[taker]) // 2
    room = jnp.where((giver == ranking[0]) | (taker == ranking[0]) | (sizes[taker] == 0), 0, jnp.maximum(room, 0))
    moved = jax.random.randint(jax.random.fold_in(own, 4), (amount // 2,), 0, 1 << 20) % (room + 1)
    sizes = sizes.at[giver].add(-moved).at[taker].add(moved)
    labels = jnp.searchsorted(jnp.cumsum(sizes), jnp.arange(rows * top), side="right").astype(jnp.int32)
    grid = labels.reshape(top, rows).T
    grid = grid[jax.random.permutation(jax.random.fold_in(own, 1), rows)]
    rotation = jax.random.randint(jax.random.fold_in(own, 2), (rows, 1), 0, top)
    return jnp.take_along_axis(grid, (jnp.arange(top)[None, :] + rotation) % top, axis=1)


def shares(amount, total, most, skew, full):
    portions = [(1 << 20) // math.isqrt(standing ** skew) + 1 for standing in range(1, amount + 1)]
    largest = most if full else min(most, max(-(-total // amount), total * portions[0] // sum(portions)))
    least = 1 if total - largest >= amount - 1 else 0
    given, rest = [largest] + [least] * (amount - 1), total - largest - least * (amount - 1)
    while rest > 0:
        movable = [i for i in range(1, amount) if given[i] < largest] or [i for i in range(1, amount) if given[i] < most]
        pool, remaining = sum([portions[i] for i in movable]), rest
        for i in movable:
            extra = min(most - given[i], max(1, remaining * portions[i] // pool), rest)
            given[i] = given[i] + extra
            rest = rest - extra
    return np.array(given)


def gaussian(own_key, extent, scale, bound, split=(), dtype=jnp.bfloat16):
    array = scale * jax.random.normal(own_key, extent, jnp.float32)
    if split:
        array = array * steps_of(own_key, extent, split, -0.22, 0.18)
    return jnp.clip(array, -bound, bound).astype(dtype)


def setup_inputs(seed: int = 0) -> dict:
    arg_keys = jax.random.split(jax.random.key(seed), 9)
    hidden_in = gaussian(arg_keys[0], (REQ, NEW_LEN, D), 1.0, 6.0, ((1, 32),))
    ln_gain = jnp.clip(1.0 + 0.18 * jax.random.normal(arg_keys[1], (D,), jnp.float32), 0.1, 1.9)
    ln_bias = gaussian(arg_keys[2], (D,), 0.5, 3.0, (), jnp.float32)
    w_qkv = gaussian(arg_keys[3], (3, D, HEADS * HD), D ** -0.5, 0.09375, ((1, 32), (2, 8)))
    w_out = gaussian(arg_keys[4], (HEADS * HD, D), HEADS ** -0.5, 1.5, ((0, 8), (1, 32)))
    cache_kv = draw_cache_kv(jax.random.fold_in(arg_keys[8], 71), 0)
    cache_len = draw_cache_len(jax.random.fold_in(arg_keys[8], 71), 0)
    owner_keys = jax.random.split(jax.random.fold_in(arg_keys[7], 1), TOKENS // TOK_DEV)
    owner_turns = jax.random.permutation(jax.random.fold_in(arg_keys[7], 3), TOKENS // TOK_DEV)
    owner = jax.vmap(lambda own, number: assign_block(jax.random.fold_in(arg_keys[7], 2), own, number, TOK_DEV, N_SEQ, 1, SLOTS, 2))(owner_keys, owner_turns).reshape((TOKENS, 1))
    return {"hidden_in": hidden_in, "ln_gain": ln_gain, "ln_bias": ln_bias, "w_qkv": w_qkv, "w_out": w_out, "cache_kv": cache_kv, "cache_len": cache_len, "owner": owner}


EPSILON = 1e-05
BASE_FREQ = 10000.0
MASKED = -1e+30

def layer_norm(values_in, gain, shift):
    wide = values_in.astype(jnp.float32)
    center = lax.optimization_barrier(jnp.mean(wide, axis=-1, keepdims=True))
    spread = wide - center
    variance = lax.optimization_barrier(jnp.mean(spread * spread, axis=-1, keepdims=True))
    return (spread * lax.rsqrt(variance + EPSILON) * gain + shift).astype(jnp.bfloat16)

def rotate(heads_in, positions):
    pair_index = jnp.arange(ROT // 2).astype(jnp.float32)
    inverse = jnp.power(BASE_FREQ, -2.0 * pair_index / ROT)
    angles = positions.astype(jnp.float32)[:, None] * inverse[None, :]
    cosine = jnp.cos(angles)[:, None, :]
    sine = jnp.sin(angles)[:, None, :]
    leading = heads_in.shape[:-1]
    paired = heads_in[..., :ROT].reshape(leading + (ROT // 2, 2))
    even = paired[..., 0]
    odd = paired[..., 1]
    turned = jnp.stack([even * cosine - odd * sine, odd * cosine + even * sine], axis=-1).reshape(leading + (ROT,))
    return jnp.concatenate([turned, heads_in[..., ROT:]], axis=-1)

def reference(hidden_in, ln_gain, ln_bias, w_qkv, w_out, cache_kv, cache_len, owner):
    normed = layer_norm(hidden_in.reshape(TOKENS, D), ln_gain, ln_bias)
    token_ids = jnp.arange(TOKENS).astype(jnp.int32)
    request = token_ids // NEW_LEN
    positions = cache_len[request] + token_ids % NEW_LEN
    shape_heads = (TOKENS, HEADS, HD)
    query = rotate(jnp.dot(normed, w_qkv[0], preferred_element_type=jnp.float32).reshape(shape_heads), positions).astype(jnp.bfloat16)
    keys_new = rotate(jnp.dot(normed, w_qkv[1], preferred_element_type=jnp.float32).reshape(shape_heads), positions).astype(jnp.bfloat16)
    values_new = jnp.dot(normed, w_qkv[2], preferred_element_type=jnp.float32).reshape(shape_heads).astype(jnp.bfloat16)
    cache_all = cache_kv.reshape(REQ, CACHE, 2, HEADS, HD)
    scale_factor = 1.0 / math.sqrt(HD)

    def one_request(which):
        start = which * NEW_LEN
        query_rows = lax.dynamic_slice_in_dim(query, start, NEW_LEN, 0).astype(jnp.float32)
        key_fresh = lax.dynamic_slice_in_dim(keys_new, start, NEW_LEN, 0)
        value_fresh = lax.dynamic_slice_in_dim(values_new, start, NEW_LEN, 0)
        cached = lax.dynamic_index_in_dim(cache_all, which, 0, keepdims=False)
        key_rows = jnp.concatenate([cached[:, 0], key_fresh], axis=0).astype(jnp.float32)
        value_rows = jnp.concatenate([cached[:, 1], value_fresh], axis=0).astype(jnp.float32)
        length = lax.dynamic_index_in_dim(cache_len, which, 0, keepdims=False)
        query_pos = length + jnp.arange(NEW_LEN).astype(jnp.int32)
        key_pos = jnp.concatenate([jnp.arange(CACHE).astype(jnp.int32), query_pos])
        usable = jnp.concatenate([jnp.arange(CACHE).astype(jnp.int32) < length, jnp.ones((NEW_LEN,), jnp.bool_)])
        allowed = usable[None, :] & (key_pos[None, :] <= query_pos[:, None])
        scores = jnp.einsum('qhd,khd->hqk', query_rows, key_rows) * scale_factor
        scores = jnp.where(allowed[None], scores, MASKED)
        highest = lax.optimization_barrier(jnp.max(scores, axis=-1, keepdims=True))
        weights = jnp.where(allowed[None], jnp.exp(scores - highest), 0.0)
        weight_sum = lax.optimization_barrier(jnp.sum(weights, axis=-1))
        rounded = lax.optimization_barrier(weights.astype(jnp.bfloat16)).astype(jnp.float32)
        mixed = jnp.einsum('hqk,khd->qhd', rounded, value_rows)
        return (mixed / jnp.transpose(weight_sum)[:, :, None]).astype(jnp.bfloat16)
    attended = lax.map(one_request, jnp.arange(REQ).astype(jnp.int32)).reshape(TOKENS, HEADS * HD)
    group_cols = HEADS * HD // N_TP

    def add_group(total, which):
        piece = lax.dynamic_slice_in_dim(attended, which * group_cols, group_cols, 1)
        weight_rows = lax.dynamic_slice_in_dim(w_out, which * group_cols, group_cols, 0)
        term = lax.optimization_barrier(jnp.dot(piece, weight_rows, preferred_element_type=jnp.float32).astype(jnp.bfloat16))
        return (total + term.astype(jnp.float32), None)
    summed, unused = lax.scan(add_group, jnp.zeros((TOKENS, D), jnp.float32), jnp.arange(N_TP).astype(jnp.int32))
    attn_out = summed.astype(jnp.bfloat16).reshape(REQ, NEW_LEN, D)
    new_dev = TOK_DEV // REQ
    fresh = jnp.stack([keys_new.reshape(TOKENS, HEADS * HD), values_new.reshape(TOKENS, HEADS * HD)], axis=1)
    fresh = fresh.reshape(REQ, N_SEQ, new_dev, 2, HEADS * HD).transpose(1, 0, 2, 3, 4).reshape(TOKENS, 2, HEADS * HD)
    owners = owner[:, 0]
    grouped = owners.reshape(N_SEQ, TOK_DEV)
    marks = (grouped[:, :, None] == jnp.arange(N_SEQ).astype(jnp.int32)[None, None, :]).astype(jnp.int32)
    earlier = jnp.cumsum(marks, axis=1) - marks
    slot_ids = lax.optimization_barrier(jnp.sum(earlier * marks, axis=-1)).reshape(TOKENS)
    sender = token_ids // TOK_DEV
    target_rows = owners * (N_SEQ * SLOTS) + sender * SLOTS + slot_ids
    appended = jnp.zeros((N_SEQ * N_SEQ * SLOTS, 2, HEADS * HD), jnp.bfloat16).at[target_rows].set(fresh)
    return (attn_out, appended)
```

```python
import jax
import jax.numpy as jnp
import numpy as np
from jax import lax
from jax.experimental import pallas as pl
from jax.experimental.pallas import tpu as pltpu
from jax.sharding import PartitionSpec as P

MESH = pl.DeviceIdType.MESH
HD = 256
ROT = 64
REQ = 4
SLOTS = 8
NZ = 8
EPSILON = 1e-05
BASE_FREQ = 10000.0
MASKED = -1e30
FAR = 1 << 20
BF = jnp.bfloat16
F32 = jnp.float32

R_WY, R_HID, R_CACHE, R_TGT = 0, 1, 3, 4
R_RING = 8
R_SIB = 24
R_Q = 40
R_KV = 44
R_FWD = 48
R_KVS = 52
R_ATT = 60
R_WOR = 68
R_WOY = 76
R_WOS = 88
R_RS = 108
R_APP = 116
N_RECV = 148
N_SEND = 160


def kernel(lens_ref, hid_ref, gain_ref, bias_ref, w_ref, wo_ref, cache_ref, cos_ref, sin_ref, kn_ref, kc_ref,
           orow_ref, ocol_ref, out_ref, app_ref,
           hido, nbuf, wbuf, acc, qs, kvs, qbuf, kvall, attin, ao, wog, pbuf, rbuf, outg, tgt,
           ssem, rsem, lsem):
    s = lax.axis_index("seq")
    t = lax.axis_index("tp")
    y = s // 16
    z = (s // 2) % NZ
    c = s % 2
    oy = 1 - y
    sg = 1 - 2 * (z % 2)
    across = y * 16 * -2 + s + 16
    sib = s + 1 - 2 * c
    t1 = t + 1 - 2 * (t % 2)

    def at_z(zz, yy=None):
        return (y if yy is None else yy) * 16 + zz * 2 + c

    zp = (z + 1) % NZ
    zm = (z + NZ - 1) % NZ
    zpair = z + sg

    barrier = pltpu.get_barrier_semaphore()

    @pl.loop(1, 32)
    def _(k):
        pl.semaphore_signal(barrier, inc=1, device_id={"seq": (s + k) % 32, "tp": t}, device_id_type=MESH)

    @pl.loop(1, 8)
    def _(k):
        pl.semaphore_signal(barrier, inc=1, device_id={"seq": s, "tp": (t + k) % 8}, device_id_type=MESH)

    pl.semaphore_signal(barrier, inc=1, device_id={"seq": across, "tp": t1}, device_id_type=MESH)
    pl.semaphore_wait(barrier, 39)

    sends = []
    locals_ = []

    def put(src, dst, r, seq, tp=None):
        copy = pltpu.make_async_remote_copy(
            src_ref=src, dst_ref=dst, send_sem=ssem.at[len(sends)], recv_sem=rsem.at[r],
            device_id={"seq": seq, "tp": t if tp is None else tp}, device_id_type=MESH)
        copy.start()
        sends.append(copy)

    def got(dst, r):
        pltpu.make_async_copy(dst, dst, rsem.at[r]).wait()

    def here(src, dst):
        copy = pltpu.make_async_copy(src, dst, lsem.at[len(locals_)])
        copy.start()
        locals_.append(copy)
        return copy

    rows_c = pl.ds(pl.multiple_of(c * 128, 128), 128)

    def wblock(yy, zz):
        return wbuf.at[yy, zz, :, rows_c, :]

    own_cols = pl.ds(pl.multiple_of(y * HD, HD), HD)
    oth_cols = pl.ds(pl.multiple_of(oy * HD, HD), HD)
    put(w_ref.at[:, :, oth_cols], wblock(y, z), R_WY, across)
    w_here = here(w_ref.at[:, :, own_cols], wblock(y, z))
    hid_here = here(hid_ref, hido.at[y])
    split = 112
    put(hid_ref.at[pl.ds(0, split)], hido.at[y, pl.ds(0, split)], R_HID, across)
    put(hid_ref.at[pl.ds(split, 256 - split)], hido.at[y, pl.ds(split, 256 - split)], R_HID + 1, across, t1)
    put(cache_ref.at[oy], kvs.at[:, y, pl.ds(64, 16), :], R_CACHE, across)
    cache_here = here(cache_ref.at[y], kvs.at[:, y, pl.ds(64, 16), :])
    wo_cols = pl.ds(pl.multiple_of(c * 128, 128), 128)
    wo_here = here(wo_ref, wog.at[y * NZ + z, :, wo_cols])

    def spread_block(yy, zz, ring, ring_sem, sib_sem):
        block = wblock(yy, zz)
        for target, r in zip(ring, ring_sem):
            put(block, block, r, at_z(target))
        put(block, block, sib_sem, sib)

    w_here.wait()
    spread_block(y, z, (zp, zm), (R_RING, R_RING + 7), R_SIB)

    def layer_norm(yy):
        def step(i, carry):
            rows = pl.ds(pl.multiple_of(i * 16, 16), 16)
            wide = hido[yy, rows, :].astype(F32)
            center = jnp.mean(wide, axis=-1, keepdims=True)
            spread = wide - center
            variance = jnp.mean(spread * spread, axis=-1, keepdims=True)
            nbuf[yy, rows, :] = (spread * lax.rsqrt(variance + EPSILON) * gain_ref[...] + bias_ref[...]).astype(BF)
            return carry
        lax.fori_loop(0, 16, step, 0)

    acc[...] = jnp.zeros_like(acc)

    order = lax.broadcasted_iota(jnp.int32, (256, 256), 0) < lax.broadcasted_iota(jnp.int32, (256, 256), 1)
    same = jnp.where(order & (ocol_ref[...] == orow_ref[...]), 1, 0)
    slot = jnp.sum(same, axis=0, keepdims=True)
    tgt[y] = jnp.broadcast_to(orow_ref[...] * 16 + y * 8 + slot, (8, 256))

    hid_here.wait()
    layer_norm(y)
    put(tgt.at[y], tgt.at[y], R_TGT, across)

    got(wblock(oy, z), R_WY)
    spread_block(oy, z, (zp, zm), (R_RING + 1, R_RING + 8), R_SIB + 1)

    def project(tok_y, yy, zz):
        offset = pl.multiple_of(yy * 2048 + zz * 256, 256)
        left = nbuf[tok_y, :, pl.ds(offset, 256)]

        def step(i, carry):
            acc[i] += jnp.dot(left, wbuf[yy, zz, i], preferred_element_type=F32)
            return carry
        lax.fori_loop(0, 3, step, 0)

    def ring_block(side, k):
        if k < 6:
            d, yy = k // 2 + 1, (y if k % 2 == 0 else oy)
        else:
            d, yy = 4, (y if side == 0 else oy)
        return yy, ((z + NZ - d) % NZ if side == 0 else (z + d) % NZ)

    def sib_wait(yy, zz, r):
        theirs = wbuf.at[yy, zz, :, pl.ds(pl.multiple_of((1 - c) * 128, 128), 128), :]
        got(theirs, r)

    waiting = [(y, z, R_SIB), (oy, z, R_SIB + 1)]
    for k in range(7):
        arrived = []
        for side in (0, 1):
            yy, zz = ring_block(side, k)
            got(wblock(yy, zz), R_RING + side * 7 + k)
            onward = None
            if k < 4:
                onward = k + 2
            elif (k == 4 and side == 0) or (k == 5 and side == 1):
                onward = 6
            ring = () if onward is None else ((zp if side == 0 else zm),)
            ring_sem = () if onward is None else (R_RING + side * 7 + onward,)
            r = R_SIB + 2 + side * 7 + k
            spread_block(yy, zz, ring, ring_sem, r)
            arrived.append((yy, zz, r))
        for yy, zz, r in waiting:
            sib_wait(yy, zz, r)
            project(y, yy, zz)
        waiting = arrived
        if k == 5:
            wo_here.wait()
            mine = wog.at[y * NZ + z, :, wo_cols]
            put(mine, mine, R_WOR, at_z(zp))
            put(mine, mine, R_WOR + 4, at_z(zm))
            put(mine, mine, R_WOY, across)
            put(mine, mine, R_WOS, sib)
            for part in (0, 1):
                rows = pl.ds(0, split) if part == 0 else pl.ds(split, 256 - split)
                got(hido.at[oy, rows], R_HID + part)
            layer_norm(oy)
    for yy, zz, r in waiting:
        sib_wait(yy, zz, r)
        project(y, yy, zz)

    lane = lax.broadcasted_iota(jnp.int32, (64, 128), 1)
    even = lane % 2 == 0

    def finish(tok_y):
        def step(r, carry):
            rows = pl.ds(pl.multiple_of(r * 64, 64), 64)
            cosine = cos_ref[tok_y, rows, :]
            sine = sin_ref[tok_y, rows, :]

            def turn(i):
                head = acc[i, rows, :]
                first = head[:, :128]
                swapped = jnp.where(even, pltpu.roll(first, 127, 1), pltpu.roll(first, 1, 1))
                return jnp.concatenate([first * cosine + swapped * sine, head[:, 128:]], axis=1).astype(BF)

            qs[r, tok_y] = turn(0)
            kvs[r, tok_y, pl.ds(0, 64), pl.ds(0, HD)] = turn(1)
            kvs[r, tok_y, pl.ds(0, 64), pl.ds(HD, HD)] = acc[2, rows, :].astype(BF)
            return carry
        lax.fori_loop(0, REQ, step, 0)

    finish(y)
    acc[...] = jnp.zeros_like(acc)

    def other(n, carry):
        project(oy, n // NZ, n % NZ)
        return carry
    lax.fori_loop(0, 16, other, 0)
    finish(oy)

    got(kvs.at[:, oy, pl.ds(64, 16), :], R_CACHE)
    cache_here.wait()
    q_here = kv_here = None
    for i, off in ((3, -3 * sg), (2, 2 * sg), (1, -sg), (0, 0)):
        dest = (z + off + NZ) % NZ
        r = dest // 2
        if i == 0:
            q_here = here(qs.at[r], qbuf.at[0])
            kv_here = here(kvs.at[r], kvall.at[c, z])
        else:
            put(kvs.at[r], kvall.at[c, z], R_KV + i, at_z(dest))
            put(qs.at[r], qbuf.at[i], R_Q + i, at_z(dest))

    def wo_slot(yy, zz, rows=None):
        return wog.at[yy * NZ + zz, (pl.ds(0, 512) if rows is None else rows), wo_cols]

    def wo_sib_slot(yy, zz, rows=None):
        cols = pl.ds(pl.multiple_of((1 - c) * 128, 128), 128)
        return wog.at[yy * NZ + zz, (pl.ds(0, 512) if rows is None else rows), cols]

    wo_sib = [(wo_sib_slot(y, z), R_WOS)]
    wo_y = [(z, None, R_WOY)]

    def wo_step(d):
        for side in (0, 1):
            zz = (z + NZ - d) % NZ if side == 0 else (z + d) % NZ
            rows = None if d < 4 else pl.ds(side * 256, 256)
            block = wo_slot(y, zz, rows)
            got(block, R_WOR + side * 4 + d - 1)
            if d < 4:
                nxt = block if d < 3 else wo_slot(y, zz, pl.ds(side * 256, 256))
                put(nxt, nxt, R_WOR + side * 4 + d, at_z(zp if side == 0 else zm))
            n = 1 + (d - 1) * 2 + side
            put(block, block, R_WOY + n, across)
            put(block, block, R_WOS + n, sib)
            wo_sib.append((wo_sib_slot(y, zz, rows), R_WOS + n))
            wo_y.append((zz, rows, R_WOY + n))

    wo_step(1)

    got(tgt.at[oy], R_TGT)
    row_id = lax.broadcasted_iota(jnp.int32, (128, 256), 0)

    def place(n, carry):
        total = jnp.zeros((128, 512), F32)
        for yy in (0, 1):
            mark = jnp.where(row_id + n * 128 == tgt[yy, 0:1, :], 1.0, 0.0).astype(BF)
            fresh = kvs[:, yy, 0:64, :].reshape(256, 512)
            total = total + jnp.dot(mark, fresh, preferred_element_type=F32)
        outg[pl.ds(n * 8, 8)] = total.astype(BF).reshape(8, 16, 512)
        return carry
    lax.fori_loop(0, 4, place, 0)
    wo_step(2)

    kv_here.wait()
    for i in range(4):
        src = (z - sg * i + NZ) % NZ
        block = kvall.at[c, src]
        if i > 0:
            got(block, R_KV + i)
        put(block, block, R_FWD + i, at_z(zpair))
        put(block, block, R_KVS + i, sib)
    wo_step(3)
    for i in range(4):
        src = (zpair + sg * i + NZ) % NZ
        block = kvall.at[c, src]
        got(block, R_FWD + i)
        put(block, block, R_KVS + 4 + i, sib)
    wo_step(4)
    for zz, rows, r in wo_y:
        block = wo_slot(oy, zz, rows)
        got(block, r)
        n = r - R_WOY
        put(block, block, R_WOS + 9 + n, sib)
        wo_sib.append((wo_sib_slot(oy, zz, rows), R_WOS + 9 + n))
    for i in range(4):
        got(kvall.at[1 - c, (z - sg * i + NZ) % NZ], R_KVS + i)
        got(kvall.at[1 - c, (zpair + sg * i + NZ) % NZ], R_KVS + 4 + i)
    q_here.wait()
    for i in range(1, 4):
        got(qbuf.at[i], R_Q + i)

    mine_r = z // 2
    length = lens_ref[mine_r]
    row = lax.broadcasted_iota(jnp.int32, (128, 1), 0)

    def attend(i):
        src = (z - sg * i + NZ) % NZ
        query = qbuf[i].reshape(128, HD)
        position = (row // 64) * 1024 + src * 128 + c * 64 + row % 64
        scores = []
        for cc in (0, 1):
            keys = kvall[cc, :, :, :, 0:HD].reshape(1280, HD)
            allowed = (kn_ref[...] + cc * 64 <= position) | (kc_ref[...] + cc * 16 < length)
            score = lax.dot_general(query, keys, (((1,), (1,)), ((), ())), preferred_element_type=F32)
            scores.append(jnp.where(allowed, score * (1.0 / 16.0), MASKED))
        top = jnp.maximum(jnp.max(scores[0], axis=1, keepdims=True), jnp.max(scores[1], axis=1, keepdims=True))
        weight_sum = jnp.zeros((128, 1), F32)
        mixed = jnp.zeros((128, HD), F32)
        for cc in (0, 1):
            weights = jnp.exp(scores[cc] - top)
            weight_sum = weight_sum + jnp.sum(weights, axis=1, keepdims=True)
            values = kvall[cc, :, :, :, HD:2 * HD].reshape(1280, HD)
            mixed = mixed + jnp.dot(weights.astype(BF), values, preferred_element_type=F32)
        ao[i] = (mixed / weight_sum).astype(BF).reshape(2, 64, HD)

    att_here = None
    head_cols = pl.ds(pl.multiple_of(y * HD, HD), HD)
    att_dst = attin.at[mine_r, :, head_cols]
    for i in (3, 2, 1, 0):
        attend(i)
        src = (z - sg * i + NZ) % NZ
        if i > 0:
            put(ao.at[i, y], att_dst, R_ATT + y * 4 + mine_r, at_z(src))
        else:
            att_here = here(ao.at[0, y], att_dst)
        put(ao.at[i, oy], att_dst, R_ATT + y * 4 + mine_r, at_z(src, oy))

    app_here = here(outg.at[s], app_ref.at[s])

    def send_app(k, start):
        dest = (s + k) % 32
        copy = pltpu.make_async_remote_copy(
            src_ref=outg.at[dest], dst_ref=app_ref.at[s], send_sem=ssem.at[N_SEND - 32 + k],
            recv_sem=rsem.at[R_APP + s], device_id={"seq": dest, "tp": t}, device_id_type=MESH)
        if start:
            copy.start()
        else:
            copy.wait_send()

    def app_go(k, carry):
        send_app(k, True)
        return carry
    lax.fori_loop(1, 32, app_go, 0)

    att_here.wait()
    for hh in (0, 1):
        for r in range(REQ):
            slot_ref = attin.at[r, :, pl.ds(hh * HD, HD)]
            mine = (r == mine_r) & (y == hh)

            @pl.when(jnp.logical_not(mine))
            def _():
                got(slot_ref, R_ATT + hh * 4 + r)
    for block, r in wo_sib:
        got(block, r)

    def partial_of(k):
        dest = (t + k) % 8
        left = attin[...].reshape(256, 512)

        def step(h, carry):
            pbuf[k, :, pl.ds(pl.multiple_of(h * 256, 256), 256)] = jnp.dot(
                left, wog[dest * 2 + h], preferred_element_type=F32).astype(BF)
            return carry
        lax.fori_loop(0, 2, step, 0)
        return dest

    for k in range(1, 8):
        dest = partial_of(k)
        put(pbuf.at[k], rbuf.at[k], R_RS + k, s, dest)
    partial_of(0)
    for k in range(1, 8):
        got(rbuf.at[k], R_RS + k)

    def total(i, carry):
        rows = pl.ds(pl.multiple_of(i * 32, 32), 32)
        value = pbuf[0, rows, :].astype(F32)
        for k in range(1, 8):
            value = value + rbuf[k, rows, :].astype(F32)
        out_ref[rows, :] = value.astype(BF)
        return carry
    lax.fori_loop(0, 8, total, 0)

    app_here.wait()

    def app_done(k, carry):
        got(app_ref.at[(s + k) % 32], R_APP + (s + k) % 32)
        send_app(k, False)
        return carry
    lax.fori_loop(1, 32, app_done, 0)
    for copy in sends:
        copy.wait_send()


def body(hidden_in, ln_gain, ln_bias, w_qkv, w_out, cache_kv, cache_len, owner):
    s = lax.axis_index("seq")
    y, zc = s // 16, s % 16
    width = w_qkv.shape[2]
    hid = hidden_in.reshape(256, hidden_in.shape[2])
    cache = jnp.transpose(cache_kv.reshape(REQ, 16, 2, 2, HD), (3, 0, 1, 2, 4)).reshape(2, REQ, 16, 512)

    ids = jnp.arange(64)
    base = (jnp.arange(2) * 16 + zc) * 64
    positions = (cache_len[None, :, None] + base[:, None, None] + ids[None, None, :]).reshape(2, 256)
    pair_index = jnp.arange(ROT // 2).astype(F32)
    inverse = jnp.power(BASE_FREQ, -2.0 * pair_index / ROT)
    angles = positions.astype(F32)[:, :, None] * jnp.repeat(inverse, 2)[None, None, :]
    sign = jnp.where(jnp.arange(ROT) % 2 == 0, -1.0, 1.0)
    cosine = jnp.concatenate([jnp.cos(angles), jnp.ones((2, 256, 64), F32)], axis=-1)
    sine = jnp.concatenate([jnp.sin(angles) * sign, jnp.zeros((2, 256, 64), F32)], axis=-1)

    u = np.arange(1280)
    j, yy, zz = u % 80, (u // 80) % 2, u // 160
    key_new = np.where(j < 64, yy * 1024 + zz * 128 + j, FAR).astype(np.int32)[None]
    key_old = np.where(j < 64, FAR, yy * 256 + zz * 32 + j - 64).astype(np.int32)[None]
    orow = owner.reshape(1, 256)
    vmem = pl.BlockSpec(memory_space=pltpu.VMEM)
    anyw = pl.BlockSpec(memory_space=pl.ANY)
    attn, app = pl.pallas_call(
        kernel,
        out_shape=(jax.ShapeDtypeStruct((256, width), BF), jax.ShapeDtypeStruct((32, 16, 512), BF)),
        in_specs=[pl.BlockSpec(memory_space=pltpu.SMEM), anyw, vmem, vmem, anyw, anyw, anyw,
                  vmem, vmem, vmem, vmem, vmem, vmem],
        out_specs=(vmem, vmem),
        scratch_shapes=[
            pltpu.VMEM((2, 256, 4096), BF),
            pltpu.VMEM((2, 256, 4096), BF),
            pltpu.VMEM((2, NZ, 3, 256, 256), BF),
            pltpu.VMEM((3, 256, 256), F32),
            pltpu.VMEM((REQ, 2, 64, HD), BF),
            pltpu.VMEM((REQ, 2, 80, 512), BF),
            pltpu.VMEM((4, 2, 64, HD), BF),
            pltpu.VMEM((2, NZ, 2, 80, 512), BF),
            pltpu.VMEM((REQ, 64, 512), BF),
            pltpu.VMEM((4, 2, 64, HD), BF),
            pltpu.VMEM((16, 512, 256), BF),
            pltpu.VMEM((8, 256, 512), BF),
            pltpu.VMEM((8, 256, 512), BF),
            pltpu.VMEM((32, 16, 512), BF),
            pltpu.VMEM((2, 8, 256), jnp.int32),
            pltpu.SemaphoreType.DMA((N_SEND,)),
            pltpu.SemaphoreType.DMA((N_RECV,)),
            pltpu.SemaphoreType.DMA((16,)),
        ],
        compiler_params=pltpu.CompilerParams(
            collective_id=0, has_side_effects=True, vmem_limit_bytes=60 * 1024 * 1024),
    )(cache_len, hid, ln_gain.reshape(1, -1), ln_bias.reshape(1, -1), w_qkv, w_out, cache,
      cosine, sine, jnp.asarray(key_new), jnp.asarray(key_old), orow, owner)
    attn_out = attn.reshape(REQ, 64, width)
    app = app.reshape(2, 16, 2, SLOTS, 2, HD)
    appended = jnp.transpose(app, (2, 1, 3, 4, 0, 5)).reshape(256, 2, width)
    return (attn_out, appended)


def solution(mesh):
    return jax.shard_map(
        body,
        mesh=mesh,
        in_specs=(
            P(None, "seq", None),
            P(),
            P(),
            P(None, "seq", "tp"),
            P("tp", "seq"),
            P(None, "seq", None, "tp"),
            P(),
            P("seq", None),
        ),
        out_specs=(P(None, "seq", "tp"), P("seq", None, "tp")),
        check_vma=False,
    )
```

```python
import jax
import jax.numpy as jnp
import numpy as np
from jax import lax
from jax.experimental import pallas as pl
from jax.experimental.pallas import tpu as pltpu
from jax.sharding import PartitionSpec as P

MESH = pl.DeviceIdType.MESH
HD = 256
ROT = 64
REQ = 4
SLOTS = 8
NZ = 8
EPSILON = 1e-05
BASE_FREQ = 10000.0
MASKED = -1e30
FAR = 1 << 20
BF = jnp.bfloat16
F32 = jnp.float32

R_WY, R_HID, R_CACHE, R_TGT = 0, 1, 3, 4
R_RING = 8
R_SIB = 24
R_Q = 40
R_KV = 44
R_FWD = 48
R_KVS = 52
R_ATT = 60
R_WOR = 68
R_WOY = 76
R_WOS = 88
R_RS = 108
R_APP = 116
N_RECV = 148
N_SEND = 160


def kernel(lens_ref, hid_ref, gain_ref, bias_ref, w_ref, wo_ref, cache_ref, freq_ref, kn_ref, kc_ref,
           orow_ref, out_ref, app_ref,
           hido, nbuf, wbuf, acc, craw, cosb, sinb, qs, kvs, qbuf, kvall, attin, ao, wog, pbuf, rbuf, outg, tgt,
           ssem, rsem, lsem):
    s = lax.axis_index("seq")
    t = lax.axis_index("tp")
    y = s // 16
    z = (s // 2) % NZ
    c = s % 2
    oy = 1 - y
    sg = 1 - 2 * (z % 2)
    across = y * 16 * -2 + s + 16
    sib = s + 1 - 2 * c
    t1 = t + 1 - 2 * (t % 2)

    def at_z(zz, yy=None):
        return (y if yy is None else yy) * 16 + zz * 2 + c

    zp = (z + 1) % NZ
    zm = (z + NZ - 1) % NZ
    zpair = z + sg

    barrier = pltpu.get_barrier_semaphore()

    @pl.loop(1, 32)
    def _(k):
        pl.semaphore_signal(barrier, inc=1, device_id={"seq": (s + k) % 32, "tp": t}, device_id_type=MESH)

    @pl.loop(1, 8)
    def _(k):
        pl.semaphore_signal(barrier, inc=1, device_id={"seq": s, "tp": (t + k) % 8}, device_id_type=MESH)

    pl.semaphore_signal(barrier, inc=1, device_id={"seq": across, "tp": t1}, device_id_type=MESH)
    pl.semaphore_wait(barrier, 39)

    sends = []
    locals_ = []

    def put(src, dst, r, seq, tp=None):
        copy = pltpu.make_async_remote_copy(
            src_ref=src, dst_ref=dst, send_sem=ssem.at[len(sends)], recv_sem=rsem.at[r],
            device_id={"seq": seq, "tp": t if tp is None else tp}, device_id_type=MESH)
        copy.start()
        sends.append(copy)

    def got(dst, r):
        pltpu.make_async_copy(dst, dst, rsem.at[r]).wait()

    def here(src, dst):
        copy = pltpu.make_async_copy(src, dst, lsem.at[len(locals_)])
        copy.start()
        locals_.append(copy)
        return copy

    rows_c = pl.ds(pl.multiple_of(c * 128, 128), 128)

    def wblock(yy, zz):
        return wbuf.at[yy, zz, :, rows_c, :]

    own_cols = pl.ds(pl.multiple_of(y * HD, HD), HD)
    oth_cols = pl.ds(pl.multiple_of(oy * HD, HD), HD)
    put(w_ref.at[:, :, oth_cols], wblock(y, z), R_WY, across)
    w_here = here(w_ref.at[:, :, own_cols], wblock(y, z))
    hid_here = here(hid_ref, hido.at[y])
    split = 112
    put(hid_ref.at[pl.ds(0, split)], hido.at[y, pl.ds(0, split)], R_HID, across)
    put(hid_ref.at[pl.ds(split, 256 - split)], hido.at[y, pl.ds(split, 256 - split)], R_HID + 1, across, t1)
    put(cache_ref.at[:, :, :, oth_cols], craw.at[y], R_CACHE, across)
    cache_here = here(cache_ref.at[:, :, :, own_cols], craw.at[y])
    wo_cols = pl.ds(pl.multiple_of(c * 128, 128), 128)
    wo_here = here(wo_ref, wog.at[y * NZ + z, :, wo_cols])

    def spread_block(yy, zz, ring, ring_sem, sib_sem):
        block = wblock(yy, zz)
        for target, r in zip(ring, ring_sem):
            put(block, block, r, at_z(target))
        put(block, block, sib_sem, sib)

    w_here.wait()
    spread_block(y, z, (zp, zm), (R_RING, R_RING + 7), R_SIB)

    def layer_norm(yy):
        def step(i, carry):
            rows = pl.ds(pl.multiple_of(i * 16, 16), 16)
            wide = hido[yy, rows, :].astype(F32)
            center = jnp.mean(wide, axis=-1, keepdims=True)
            spread = wide - center
            variance = jnp.mean(spread * spread, axis=-1, keepdims=True)
            nbuf[yy, rows, :] = (spread * lax.rsqrt(variance + EPSILON) * gain_ref[...] + bias_ref[...]).astype(BF)
            return carry
        lax.fori_loop(0, 16, step, 0)

    acc[...] = jnp.zeros_like(acc)

    def tables():
        spot = lax.broadcasted_iota(jnp.int32, (64, 128), 0)
        odd = lax.broadcasted_iota(jnp.int32, (64, 128), 1) % 2
        for yy in (0, 1):
            for r in range(REQ):
                position = spot + (lens_ref[r] + yy * 1024 + z * 128 + c * 64)
                angle = position.astype(F32) * freq_ref[...]
                cosb[yy, pl.ds(r * 64, 64), :] = jnp.cos(angle)
                turned = jnp.sin(angle)
                sinb[yy, pl.ds(r * 64, 64), :] = jnp.where(odd == 1, turned, -turned)
        before = lax.broadcasted_iota(jnp.int32, (256, 256), 0) < lax.broadcasted_iota(jnp.int32, (256, 256), 1)
        across_lanes = jnp.broadcast_to(orow_ref[...].astype(F32), (256, 256))
        same = jnp.where(before & (jnp.transpose(across_lanes) == across_lanes), 1, 0)
        slot = jnp.sum(same, axis=0, keepdims=True)
        tgt[y] = jnp.broadcast_to(orow_ref[...] * 16 + y * 8 + slot, (8, 256))

    got(wblock(oy, z), R_WY)
    spread_block(oy, z, (zp, zm), (R_RING + 1, R_RING + 8), R_SIB + 1)
    hid_here.wait()
    layer_norm(y)

    def project(tok_y, yy, zz):
        offset = pl.multiple_of(yy * 2048 + zz * 256, 256)
        left = nbuf[tok_y, :, pl.ds(offset, 256)]

        def step(i, carry):
            acc[tok_y, i] += jnp.dot(left, wbuf[yy, zz, i], preferred_element_type=F32)
            return carry
        lax.fori_loop(0, 3, step, 0)

    def ring_block(side, k):
        if k < 6:
            d, yy = k // 2 + 1, (y if k % 2 == 0 else oy)
        else:
            d, yy = 4, (y if side == 0 else oy)
        return yy, ((z + NZ - d) % NZ if side == 0 else (z + d) % NZ)

    def sib_wait(yy, zz, r):
        theirs = wbuf.at[yy, zz, :, pl.ds(pl.multiple_of((1 - c) * 128, 128), 128), :]
        got(theirs, r)

    waiting = [(y, z, R_SIB), (oy, z, R_SIB + 1)]
    for k in range(7):
        arrived = []
        for side in (0, 1):
            yy, zz = ring_block(side, k)
            got(wblock(yy, zz), R_RING + side * 7 + k)
            onward = None
            if k < 4:
                onward = k + 2
            elif (k == 4 and side == 0) or (k == 5 and side == 1):
                onward = 6
            ring = () if onward is None else ((zp if side == 0 else zm),)
            ring_sem = () if onward is None else (R_RING + side * 7 + onward,)
            r = R_SIB + 2 + side * 7 + k
            spread_block(yy, zz, ring, ring_sem, r)
            arrived.append((yy, zz, r))
        for yy, zz, r in waiting:
            sib_wait(yy, zz, r)
            project(y, yy, zz)
        waiting = arrived
        if k == 0:
            tables()
            put(tgt.at[y], tgt.at[y], R_TGT, across)
        if k == 2:
            got(craw.at[oy], R_CACHE)
            cache_here.wait()
            for yy in (0, 1):
                raw = craw[yy]
                kvs[:, yy, 64:80, 0:HD] = raw[:, :, 0, :]
                kvs[:, yy, 64:80, HD:2 * HD] = raw[:, :, 1, :]
        if k == 4:
            for part in (0, 1):
                rows = pl.ds(0, split) if part == 0 else pl.ds(split, 256 - split)
                got(hido.at[oy, rows], R_HID + part)
            layer_norm(oy)
        if k == 5:
            wo_here.wait()
            mine = wog.at[y * NZ + z, :, wo_cols]
            put(mine, mine, R_WOR, at_z(zp))
            put(mine, mine, R_WOR + 4, at_z(zm))
            put(mine, mine, R_WOY, across)
            put(mine, mine, R_WOS, sib)

            def catch_up(n, carry):
                project(oy, n % 2, (z + NZ - 2 + n // 2) % NZ)
                return carry
            lax.fori_loop(0, 10, catch_up, 0)
            for d in (3, NZ - 3):
                project(oy, y, (z + d) % NZ)
    for yy, zz in ((oy, (z + NZ - 3) % NZ), (oy, (z + 3) % NZ)):
        project(oy, yy, zz)
    for yy, zz, r in waiting:
        sib_wait(yy, zz, r)
        project(y, yy, zz)
        project(oy, yy, zz)

    lane = lax.broadcasted_iota(jnp.int32, (64, 128), 1)
    even = lane % 2 == 0

    def finish(tok_y):
        def step(r, carry):
            rows = pl.ds(pl.multiple_of(r * 64, 64), 64)
            cosine = cosb[tok_y, rows, :]
            sine = sinb[tok_y, rows, :]

            def turn(i):
                head = acc[tok_y, i, rows, :]
                first = head[:, :128]
                swapped = jnp.where(even, pltpu.roll(first, 127, 1), pltpu.roll(first, 1, 1))
                return jnp.concatenate([first * cosine + swapped * sine, head[:, 128:]], axis=1).astype(BF)

            qs[r, tok_y] = turn(0)
            kvs[r, tok_y, pl.ds(0, 64), pl.ds(0, HD)] = turn(1)
            kvs[r, tok_y, pl.ds(0, 64), pl.ds(HD, HD)] = acc[tok_y, 2, rows, :].astype(BF)
            return carry
        lax.fori_loop(0, REQ, step, 0)

    finish(y)
    finish(oy)

    q_here = kv_here = None
    for i, off in ((3, -3 * sg), (2, 2 * sg), (1, -sg), (0, 0)):
        dest = (z + off + NZ) % NZ
        r = dest // 2
        if i == 0:
            q_here = here(qs.at[r], qbuf.at[0])
            kv_here = here(kvs.at[r], kvall.at[c, z])
        else:
            put(kvs.at[r], kvall.at[c, z], R_KV + i, at_z(dest))
            put(qs.at[r], qbuf.at[i], R_Q + i, at_z(dest))

    def wo_slot(yy, zz, rows=None):
        return wog.at[yy * NZ + zz, (pl.ds(0, 512) if rows is None else rows), wo_cols]

    def wo_sib_slot(yy, zz, rows=None):
        cols = pl.ds(pl.multiple_of((1 - c) * 128, 128), 128)
        return wog.at[yy * NZ + zz, (pl.ds(0, 512) if rows is None else rows), cols]

    wo_sib = [(wo_sib_slot(y, z), R_WOS)]
    wo_y = [(z, None, R_WOY)]

    def wo_step(d):
        for side in (0, 1):
            zz = (z + NZ - d) % NZ if side == 0 else (z + d) % NZ
            rows = None if d < 4 else pl.ds(side * 256, 256)
            block = wo_slot(y, zz, rows)
            got(block, R_WOR + side * 4 + d - 1)
            if d < 4:
                nxt = block if d < 3 else wo_slot(y, zz, pl.ds(side * 256, 256))
                put(nxt, nxt, R_WOR + side * 4 + d, at_z(zp if side == 0 else zm))
            n = 1 + (d - 1) * 2 + side
            put(block, block, R_WOY + n, across)
            put(block, block, R_WOS + n, sib)
            wo_sib.append((wo_sib_slot(y, zz, rows), R_WOS + n))
            wo_y.append((zz, rows, R_WOY + n))

    wo_step(1)

    got(tgt.at[oy], R_TGT)
    row_id = lax.broadcasted_iota(jnp.int32, (256, 256), 0)

    def place(n, carry):
        total = jnp.zeros((256, HD), F32)
        for yy in (0, 1):
            for kv in (0, 1):
                mark = jnp.where(row_id + n * 256 == tgt[yy, 0:1, :] * 2 + kv, 1.0, 0.0).astype(BF)
                fresh = kvs[:, yy, 0:64, kv * HD:(kv + 1) * HD].reshape(256, HD)
                total = total + jnp.dot(mark, fresh, preferred_element_type=F32)
        outg[pl.ds(n * 8, 8)] = total.reshape(8, 2, SLOTS, 2, HD).astype(BF)
        return carry
    lax.fori_loop(0, 4, place, 0)

    kv_here.wait()
    for i in range(4):
        src = (z - sg * i + NZ) % NZ
        block = kvall.at[c, src]
        if i > 0:
            got(block, R_KV + i)
        put(block, block, R_FWD + i, at_z(zpair))
        put(block, block, R_KVS + i, sib)
    wo_step(2)
    for i in range(4):
        src = (zpair + sg * i + NZ) % NZ
        block = kvall.at[c, src]
        got(block, R_FWD + i)
        put(block, block, R_KVS + 4 + i, sib)
    wo_step(3)

    def wo_onward(which):
        for zz, rows, r in which:
            block = wo_slot(oy, zz, rows)
            got(block, r)
            n = r - R_WOY
            put(block, block, R_WOS + 9 + n, sib)
            wo_sib.append((wo_sib_slot(oy, zz, rows), R_WOS + 9 + n))

    for i in range(4):
        got(kvall.at[1 - c, (z - sg * i + NZ) % NZ], R_KVS + i)
        got(kvall.at[1 - c, (zpair + sg * i + NZ) % NZ], R_KVS + 4 + i)
    q_here.wait()
    for i in range(1, 4):
        got(qbuf.at[i], R_Q + i)

    mine_r = z // 2
    length = lens_ref[mine_r]
    row = lax.broadcasted_iota(jnp.int32, (128, 1), 0)

    def attend(i):
        src = (z - sg * i + NZ) % NZ
        query = qbuf[i].reshape(128, HD)
        position = (row // 64) * 1024 + src * 128 + c * 64 + row % 64
        scores = []
        for cc in (0, 1):
            keys = kvall[cc, :, :, :, 0:HD].reshape(1280, HD)
            allowed = (kn_ref[...] + cc * 64 <= position) | (kc_ref[...] + cc * 16 < length)
            score = lax.dot_general(query, keys, (((1,), (1,)), ((), ())), preferred_element_type=F32)
            scores.append(jnp.where(allowed, score * (1.0 / 16.0), MASKED))
        top = jnp.maximum(jnp.max(scores[0], axis=1, keepdims=True), jnp.max(scores[1], axis=1, keepdims=True))
        weight_sum = jnp.zeros((128, 1), F32)
        mixed = jnp.zeros((128, HD), F32)
        for cc in (0, 1):
            weights = jnp.exp(scores[cc] - top)
            weight_sum = weight_sum + jnp.sum(weights, axis=1, keepdims=True)
            values = kvall[cc, :, :, :, HD:2 * HD].reshape(1280, HD)
            mixed = mixed + jnp.dot(weights.astype(BF), values, preferred_element_type=F32)
        ao[i] = (mixed / weight_sum).astype(BF).reshape(2, 64, HD)

    att_here = None
    head_cols = pl.ds(pl.multiple_of(y * HD, HD), HD)
    att_dst = attin.at[mine_r, :, head_cols]
    for i in (3, 2, 1, 0):
        attend(i)
        src = (z - sg * i + NZ) % NZ
        if i > 0:
            put(ao.at[i, y], att_dst, R_ATT + y * 4 + mine_r, at_z(src))
        else:
            att_here = here(ao.at[0, y], att_dst)
        put(ao.at[i, oy], att_dst, R_ATT + y * 4 + mine_r, at_z(src, oy))
        if i == 3:
            wo_step(4)
        if i == 2:
            wo_onward(wo_y[:5])

    head_cols_of = pl.ds(pl.multiple_of(y * HD, HD), HD)
    app_here = here(outg.at[s], app_ref.at[:, s % 16, :, :, head_cols_of])

    def send_app(k, start):
        dest = (s + k) % 32
        copy = pltpu.make_async_remote_copy(
            src_ref=outg.at[dest], dst_ref=app_ref.at[:, s % 16, :, :, head_cols_of], send_sem=ssem.at[N_SEND - 32 + k],
            recv_sem=rsem.at[R_APP + s], device_id={"seq": dest, "tp": t}, device_id_type=MESH)
        if start:
            copy.start()
        else:
            copy.wait_send()

    def app_go(k, carry):
        send_app(k, True)
        return carry
    lax.fori_loop(1, 32, app_go, 0)

    att_here.wait()
    for hh in (0, 1):
        for r in range(REQ):
            slot_ref = attin.at[r, :, pl.ds(hh * HD, HD)]
            mine = (r == mine_r) & (y == hh)

            @pl.when(jnp.logical_not(mine))
            def _():
                got(slot_ref, R_ATT + hh * 4 + r)
    wo_onward(wo_y[5:])
    for block, r in wo_sib:
        got(block, r)

    def partial_of(k):
        dest = (t + k) % 8
        left = attin[...].reshape(256, 512)

        def step(h, carry):
            pbuf[k, :, pl.ds(pl.multiple_of(h * 256, 256), 256)] = jnp.dot(
                left, wog[dest * 2 + h], preferred_element_type=F32).astype(BF)
            return carry
        lax.fori_loop(0, 2, step, 0)
        return dest

    for k in range(1, 8):
        dest = partial_of(k)
        put(pbuf.at[k], rbuf.at[k], R_RS + k, s, dest)
    partial_of(0)
    for k in range(1, 8):
        got(rbuf.at[k], R_RS + k)

    def total(i, carry):
        rows = pl.ds(pl.multiple_of(i * 32, 32), 32)
        value = pbuf[0, rows, :].astype(F32)
        for k in range(1, 8):
            value = value + rbuf[k, rows, :].astype(F32)
        out_ref[rows, :] = value.astype(BF)
        return carry
    lax.fori_loop(0, 8, total, 0)

    app_here.wait()

    def app_done(k, carry):
        o = (s + k) % 32
        cols = pl.ds(pl.multiple_of(o // 16 * HD, HD), HD)
        got(app_ref.at[:, o % 16, :, :, cols], R_APP + o)
        send_app(k, False)
        return carry
    lax.fori_loop(1, 32, app_done, 0)
    for copy in sends:
        copy.wait_send()


def body(hidden_in, ln_gain, ln_bias, w_qkv, w_out, cache_kv, cache_len, owner):
    width = w_qkv.shape[2]
    hid = hidden_in.reshape(256, hidden_in.shape[2])
    pair = np.arange(128) // 2
    freq = np.where(pair < ROT // 2, BASE_FREQ ** (-2.0 * pair / ROT), 0.0).astype(np.float32)[None]
    u = np.arange(1280)
    j, yy, zz = u % 80, (u // 80) % 2, u // 160
    key_new = np.where(j < 64, yy * 1024 + zz * 128 + j, FAR).astype(np.int32)[None]
    key_old = np.where(j < 64, FAR, yy * 256 + zz * 32 + j - 64).astype(np.int32)[None]
    orow = owner.reshape(1, 256)
    vmem = pl.BlockSpec(memory_space=pltpu.VMEM)
    anyw = pl.BlockSpec(memory_space=pl.ANY)
    attn, app = pl.pallas_call(
        kernel,
        out_shape=(jax.ShapeDtypeStruct((256, width), BF), jax.ShapeDtypeStruct((2, 16, SLOTS, 2, width), BF)),
        in_specs=[pl.BlockSpec(memory_space=pltpu.SMEM), anyw, vmem, vmem, anyw, anyw, anyw,
                  vmem, vmem, vmem, vmem],
        out_specs=(vmem, vmem),
        scratch_shapes=[
            pltpu.VMEM((2, 256, 4096), BF),
            pltpu.VMEM((2, 256, 4096), BF),
            pltpu.VMEM((2, NZ, 3, 256, 256), BF),
            pltpu.VMEM((2, 3, 256, 256), F32),
            pltpu.VMEM((2, REQ, 16, 2, HD), BF),
            pltpu.VMEM((2, 256, 128), F32),
            pltpu.VMEM((2, 256, 128), F32),
            pltpu.VMEM((REQ, 2, 64, HD), BF),
            pltpu.VMEM((REQ, 2, 80, 512), BF),
            pltpu.VMEM((4, 2, 64, HD), BF),
            pltpu.VMEM((2, NZ, 2, 80, 512), BF),
            pltpu.VMEM((REQ, 64, 512), BF),
            pltpu.VMEM((4, 2, 64, HD), BF),
            pltpu.VMEM((16, 512, 256), BF),
            pltpu.VMEM((8, 256, 512), BF),
            pltpu.VMEM((8, 256, 512), BF),
            pltpu.VMEM((32, 2, SLOTS, 2, HD), BF),
            pltpu.VMEM((2, 8, 256), jnp.int32),
            pltpu.SemaphoreType.DMA((N_SEND,)),
            pltpu.SemaphoreType.DMA((N_RECV,)),
            pltpu.SemaphoreType.DMA((16,)),
        ],
        compiler_params=pltpu.CompilerParams(
            collective_id=0, has_side_effects=True, vmem_limit_bytes=60 * 1024 * 1024),
    )(cache_len, hid, ln_gain.reshape(1, -1), ln_bias.reshape(1, -1), w_qkv, w_out, cache_kv,
      jnp.asarray(freq), jnp.asarray(key_new), jnp.asarray(key_old), orow)
    attn_out = attn.reshape(REQ, 64, width)
    appended = app.reshape(256, 2, width)
    return (attn_out, appended)


def solution(mesh):
    return jax.shard_map(
        body,
        mesh=mesh,
        in_specs=(
            P(None, "seq", None),
            P(),
            P(),
            P(None, "seq", "tp"),
            P("tp", "seq"),
            P(None, "seq", None, "tp"),
            P(),
            P("seq", None),
        ),
        out_specs=(P(None, "seq", "tp"), P("seq", None, "tp")),
        check_vma=False,
    )
```

```python
import jax
import jax.numpy as jnp
import numpy as np
from jax import lax
from jax.experimental import pallas as pl
from jax.experimental.pallas import tpu as pltpu
from jax.sharding import PartitionSpec as P

MESH = pl.DeviceIdType.MESH
HD = 256
ROT = 64
REQ = 4
SLOTS = 8
NZ = 8
EPSILON = 1e-05
BASE_FREQ = 10000.0
MASKED = -1e30
FAR = 1 << 20
BF = jnp.bfloat16
F32 = jnp.float32

R_WY, R_CACHE, R_TGT, R_HID = 0, 1, 2, 4
R_RING = 8
R_SIB = 22
R_Q = 38
R_KV = 46
R_FWD = 54
R_KVS = 62
R_ATT = 78
R_WOR = 86
R_WOY = 94
R_WOS = 103
R_RS = 121
R_APP = 129
N_RECV = 161
N_SEND = 192


def kernel(lens_ref, hid_ref, gain_ref, bias_ref, w_ref, wo_ref, cache_ref, freq_ref, kn_ref, kc_ref,
           orow_ref, out_ref, app_ref,
           hido, nbuf, wbuf, acc, craw, cosb, sinb, qs, kvs, qbuf, kvall, attin, ao, wog, pbuf, rbuf, outg, tgt,
           ssem, rsem, lsem):
    s = lax.axis_index("seq")
    t = lax.axis_index("tp")
    y = s // 16
    z = (s // 2) % NZ
    c = s % 2
    oy = 1 - y
    sg = 1 - 2 * (z % 2)
    across = y * 16 * -2 + s + 16
    sib = s + 1 - 2 * c
    t1 = t + 1 - 2 * (t % 2)

    def at_z(zz, yy=None):
        return (y if yy is None else yy) * 16 + zz * 2 + c

    zp = (z + 1) % NZ
    zm = (z + NZ - 1) % NZ
    zpair = z + sg

    barrier = pltpu.get_barrier_semaphore()

    @pl.loop(1, 32)
    def _(k):
        pl.semaphore_signal(barrier, inc=1, device_id={"seq": (s + k) % 32, "tp": t}, device_id_type=MESH)

    @pl.loop(1, 8)
    def _(k):
        pl.semaphore_signal(barrier, inc=1, device_id={"seq": s, "tp": (t + k) % 8}, device_id_type=MESH)

    pl.semaphore_signal(barrier, inc=1, device_id={"seq": across, "tp": t1}, device_id_type=MESH)
    pl.semaphore_wait(barrier, 39)

    sends = []
    locals_ = []

    def put(src, dst, r, seq, tp=None):
        copy = pltpu.make_async_remote_copy(
            src_ref=src, dst_ref=dst, send_sem=ssem.at[len(sends)], recv_sem=rsem.at[r],
            device_id={"seq": seq, "tp": t if tp is None else tp}, device_id_type=MESH)
        copy.start()
        sends.append(copy)

    def got(dst, r):
        pltpu.make_async_copy(dst, dst, rsem.at[r]).wait()

    def here(src, dst):
        copy = pltpu.make_async_copy(src, dst, lsem.at[len(locals_)])
        copy.start()
        locals_.append(copy)
        return copy

    rows_c = pl.ds(pl.multiple_of(c * 128, 128), 128)

    def wblock(yy, zz):
        return wbuf.at[yy, zz, :, rows_c, :]

    own_cols = pl.ds(pl.multiple_of(y * HD, HD), HD)
    oth_cols = pl.ds(pl.multiple_of(oy * HD, HD), HD)
    put(w_ref.at[:, :, oth_cols], wblock(y, z), R_WY, across)
    w_here = here(w_ref.at[:, :, own_cols], wblock(y, z))
    hid_here = here(hid_ref, hido.at[y])
    hid_rows = ((0, 64, t), (64, 64, t1), (128, 48, t), (176, 80, t1))
    for n, (first, count, via) in enumerate(hid_rows):
        put(hid_ref.at[pl.ds(first, count)], hido.at[y, pl.ds(first, count)], R_HID + n, across, via)
    put(cache_ref.at[:, :, :, oth_cols], craw.at[y], R_CACHE, across)
    cache_here = here(cache_ref.at[:, :, :, own_cols], craw.at[y])
    wo_cols = pl.ds(pl.multiple_of(c * 128, 128), 128)
    wo_here = here(wo_ref, wog.at[y * NZ + z, :, wo_cols])

    def spread_block(yy, zz, ring, ring_sem, sib_sem):
        block = wblock(yy, zz)
        for target, r in zip(ring, ring_sem):
            put(block, block, r, at_z(target))
        put(block, block, sib_sem, sib)

    w_here.wait()
    spread_block(y, z, (zp, zm), (R_RING, R_RING + 7), R_SIB)

    def layer_norm(yy, first=0, count=256):
        def step(i, carry):
            rows = pl.ds(pl.multiple_of(i * 16, 16), 16)
            wide = hido[yy, rows, :].astype(F32)
            center = jnp.mean(wide, axis=-1, keepdims=True)
            spread = wide - center
            variance = jnp.mean(spread * spread, axis=-1, keepdims=True)
            nbuf[yy, rows, :] = (spread * lax.rsqrt(variance + EPSILON) * gain_ref[...] + bias_ref[...]).astype(BF)
            return carry
        lax.fori_loop(first // 16, (first + count) // 16, step, 0)

    acc[...] = jnp.zeros_like(acc)

    def tables():
        spot = lax.broadcasted_iota(jnp.int32, (64, 128), 0)
        odd = lax.broadcasted_iota(jnp.int32, (64, 128), 1) % 2
        for yy in (0, 1):
            for r in range(REQ):
                position = spot + (lens_ref[r] + yy * 1024 + z * 128 + c * 64)
                angle = position.astype(F32) * freq_ref[...]
                cosb[yy, pl.ds(r * 64, 64), :] = jnp.cos(angle)
                turned = jnp.sin(angle)
                sinb[yy, pl.ds(r * 64, 64), :] = jnp.where(odd == 1, turned, -turned)
        before = lax.broadcasted_iota(jnp.int32, (256, 256), 0) < lax.broadcasted_iota(jnp.int32, (256, 256), 1)
        across_lanes = jnp.broadcast_to(orow_ref[...].astype(F32), (256, 256))
        same = jnp.where(before & (jnp.transpose(across_lanes) == across_lanes), 1, 0)
        slot = jnp.sum(same, axis=0, keepdims=True)
        tgt[y] = jnp.broadcast_to(orow_ref[...] * 16 + y * 8 + slot, (8, 256))

    got(wblock(oy, z), R_WY)
    spread_block(oy, z, (zp, zm), (R_RING + 1, R_RING + 8), R_SIB + 1)
    hid_here.wait()
    layer_norm(y)

    def project(tok_y, yy, zz, first=0, count=256):
        offset = pl.multiple_of(yy * 2048 + zz * 256, 256)
        rows = pl.ds(first, count)
        left = nbuf[tok_y, rows, pl.ds(offset, 256)]

        for i in range(3):
            acc[tok_y, i, rows, :] += jnp.dot(left, wbuf[yy, zz, i], preferred_element_type=F32)

    def ring_block(side, k):
        if k < 6:
            d, yy = k // 2 + 1, (y if k % 2 == 0 else oy)
        else:
            d, yy = 4, (y if side == 0 else oy)
        return yy, ((z + NZ - d) % NZ if side == 0 else (z + d) % NZ)

    def sib_wait(yy, zz, r):
        theirs = wbuf.at[yy, zz, :, pl.ds(pl.multiple_of((1 - c) * 128, 128), 128), :]
        got(theirs, r)

    waiting = [(y, z, R_SIB), (oy, z, R_SIB + 1)]
    for k in range(7):
        arrived = []
        for side in (0, 1):
            yy, zz = ring_block(side, k)
            got(wblock(yy, zz), R_RING + side * 7 + k)
            onward = None
            if k < 4:
                onward = k + 2
            elif (k == 4 and side == 0) or (k == 5 and side == 1):
                onward = 6
            ring = () if onward is None else ((zp if side == 0 else zm),)
            ring_sem = () if onward is None else (R_RING + side * 7 + onward,)
            r = R_SIB + 2 + side * 7 + k
            spread_block(yy, zz, ring, ring_sem, r)
            arrived.append((yy, zz, r))
        for yy, zz, r in waiting:
            sib_wait(yy, zz, r)
            project(y, yy, zz)
        waiting = arrived
        if k == 0:
            tables()
            put(tgt.at[y], tgt.at[y], R_TGT, across)
        if k == 2:
            got(craw.at[oy], R_CACHE)
            cache_here.wait()
            for yy in (0, 1):
                raw = craw[yy]
                kvs[:, yy, 64:80, 0:HD] = raw[:, :, 0, :]
                kvs[:, yy, 64:80, HD:2 * HD] = raw[:, :, 1, :]
        if k == 3 or k == 5:
            n = k - 3
            if k == 5:
                wo_here.wait()
                mine = wog.at[y * NZ + z, :, wo_cols]
                put(mine, mine, R_WOR, at_z(zp))
                put(mine, mine, R_WOR + 4, at_z(zm))
                put(mine, mine, R_WOY, across)
                put(mine, mine, R_WOS, sib)
            for part in (n, n + 1):
                first, count, _ = hid_rows[part]
                got(hido.at[oy, pl.ds(first, count)], R_HID + part)
            layer_norm(oy, n * 64, 128)
        if k == 4 or k == 5:
            half = (k - 4) * 128

            def catch_up(n, carry):
                project(oy, n % 2, (z + NZ - 2 + n // 2) % NZ, half, 128)
                return carry
            lax.fori_loop(0, 10, catch_up, 0)
        if k == 5:
            for d in (3, NZ - 3):
                project(oy, y, (z + d) % NZ)
    for yy, zz, r in waiting:
        sib_wait(yy, zz, r)
        project(y, yy, zz)

    lane = lax.broadcasted_iota(jnp.int32, (64, 128), 1)
    even = lane % 2 == 0

    def finish(tok_y):
        def step(r, carry):
            rows = pl.ds(pl.multiple_of(r * 64, 64), 64)
            cosine = cosb[tok_y, rows, :]
            sine = sinb[tok_y, rows, :]

            def turn(i):
                head = acc[tok_y, i, rows, :]
                first = head[:, :128]
                swapped = jnp.where(even, pltpu.roll(first, 127, 1), pltpu.roll(first, 1, 1))
                return jnp.concatenate([first * cosine + swapped * sine, head[:, 128:]], axis=1).astype(BF)

            qs[r, tok_y] = turn(0)
            kvs[r, tok_y, pl.ds(0, 64), pl.ds(0, HD)] = turn(1)
            kvs[r, tok_y, pl.ds(0, 64), pl.ds(HD, HD)] = acc[tok_y, 2, rows, :].astype(BF)
            return carry
        lax.fori_loop(0, REQ, step, 0)

    def send_round(h, yy):
        held = []
        hops = ((3, (z - 3 * sg + NZ) % NZ), (2, (z + 2 * sg + NZ) % NZ), (1, (z - sg + NZ) % NZ))
        for i, dest in hops:
            put(kvs.at[dest // 2, yy], kvall.at[c, z, yy], R_KV + h * 4 + i, at_z(dest))
        for i, dest in hops:
            put(qs.at[dest // 2, yy], qbuf.at[i, yy], R_Q + h * 4 + i, at_z(dest))
        held.append(here(kvs.at[z // 2, yy], kvall.at[c, z, yy]))
        held.append(here(qs.at[z // 2, yy], qbuf.at[0, yy]))
        return held

    def forward_round(h, yy, held):
        held[0].wait()
        for i in range(4):
            block = kvall.at[c, (z - sg * i + NZ) % NZ, yy]
            if i > 0:
                got(block, R_KV + h * 4 + i)
            put(block, block, R_FWD + h * 4 + i, at_z(zpair))
            put(block, block, R_KVS + h * 8 + i, sib)

    def sibling_round(h, yy):
        for i in range(4):
            block = kvall.at[c, (zpair + sg * i + NZ) % NZ, yy]
            got(block, R_FWD + h * 4 + i)
            put(block, block, R_KVS + h * 8 + 4 + i, sib)

    finish(y)
    held_own = send_round(0, y)
    for yy, zz in ((oy, (z + NZ - 3) % NZ), (oy, (z + 3) % NZ)):
        project(oy, yy, zz)
    for yy, zz, r in waiting:
        project(oy, yy, zz)
    finish(oy)
    held_oth = send_round(1, oy)

    def wo_slot(yy, zz, rows=None):
        return wog.at[yy * NZ + zz, (pl.ds(0, 512) if rows is None else rows), wo_cols]

    def wo_sib_slot(yy, zz, rows=None):
        cols = pl.ds(pl.multiple_of((1 - c) * 128, 128), 128)
        return wog.at[yy * NZ + zz, (pl.ds(0, 512) if rows is None else rows), cols]

    wo_sib = [(wo_sib_slot(y, z), R_WOS)]
    wo_y = [(z, None, R_WOY)]

    def wo_step(d):
        for side in (0, 1):
            zz = (z + NZ - d) % NZ if side == 0 else (z + d) % NZ
            rows = None if d < 4 else pl.ds(side * 256, 256)
            block = wo_slot(y, zz, rows)
            got(block, R_WOR + side * 4 + d - 1)
            if d < 4:
                nxt = block if d < 3 else wo_slot(y, zz, pl.ds(side * 256, 256))
                put(nxt, nxt, R_WOR + side * 4 + d, at_z(zp if side == 0 else zm))
            n = 1 + (d - 1) * 2 + side
            put(block, block, R_WOY + n, across)
            put(block, block, R_WOS + n, sib)
            wo_sib.append((wo_sib_slot(y, zz, rows), R_WOS + n))
            wo_y.append((zz, rows, R_WOY + n))

    wo_step(1)
    forward_round(0, y, held_own)

    got(tgt.at[oy], R_TGT)
    row_id = lax.broadcasted_iota(jnp.int32, (256, 256), 0)

    def place(n, carry):
        total = jnp.zeros((256, HD), F32)
        for yy in (0, 1):
            for kv in (0, 1):
                mark = jnp.where(row_id + n * 256 == tgt[yy, 0:1, :] * 2 + kv, 1.0, 0.0).astype(BF)
                fresh = kvs[:, yy, 0:64, kv * HD:(kv + 1) * HD].reshape(256, HD)
                total = total + jnp.dot(mark, fresh, preferred_element_type=F32)
        outg[pl.ds(n * 8, 8)] = total.reshape(8, 2, SLOTS, 2, HD).astype(BF)
        return carry
    lax.fori_loop(0, 4, place, 0)

    sibling_round(0, y)
    forward_round(1, oy, held_oth)
    wo_step(2)
    sibling_round(1, oy)
    wo_step(3)

    def wo_onward(which):
        for zz, rows, r in which:
            block = wo_slot(oy, zz, rows)
            got(block, r)
            n = r - R_WOY
            put(block, block, R_WOS + 9 + n, sib)
            wo_sib.append((wo_sib_slot(oy, zz, rows), R_WOS + 9 + n))

    for h, yy in ((0, y), (1, oy)):
        for i in range(4):
            got(kvall.at[1 - c, (z - sg * i + NZ) % NZ, yy], R_KVS + h * 8 + i)
            got(kvall.at[1 - c, (zpair + sg * i + NZ) % NZ, yy], R_KVS + h * 8 + 4 + i)
            if i > 0:
                got(qbuf.at[i, yy], R_Q + h * 4 + i)
    held_own[1].wait()
    held_oth[1].wait()

    head_cols_of = pl.ds(pl.multiple_of(y * HD, HD), HD)

    def send_app(n, start):
        dest = jnp.where(n < 16, oy, y) * 16 + (s + n) % 16
        copy = pltpu.make_async_remote_copy(
            src_ref=outg.at[dest], dst_ref=app_ref.at[:, s % 16, :, :, head_cols_of],
            send_sem=ssem.at[N_SEND - 32 + n], recv_sem=rsem.at[R_APP + s],
            device_id={"seq": dest, "tp": t}, device_id_type=MESH)
        if start:
            copy.start()
        else:
            copy.wait_send()

    def app_go(n, carry):
        send_app(n, True)
        return carry
    lax.fori_loop(0, 16, app_go, 0)

    mine_r = z // 2
    length = lens_ref[mine_r]
    row = lax.broadcasted_iota(jnp.int32, (128, 1), 0)

    def attend(i):
        src = (z - sg * i + NZ) % NZ
        query = qbuf[i].reshape(128, HD)
        position = (row // 64) * 1024 + src * 128 + c * 64 + row % 64
        scores = []
        for cc in (0, 1):
            keys = kvall[cc, :, :, :, 0:HD].reshape(1280, HD)
            allowed = (kn_ref[...] + cc * 64 <= position) | (kc_ref[...] + cc * 16 < length)
            score = lax.dot_general(query, keys, (((1,), (1,)), ((), ())), preferred_element_type=F32)
            scores.append(jnp.where(allowed, score * (1.0 / 16.0), MASKED))
        top = jnp.maximum(jnp.max(scores[0], axis=1, keepdims=True), jnp.max(scores[1], axis=1, keepdims=True))
        weight_sum = jnp.zeros((128, 1), F32)
        mixed = jnp.zeros((128, HD), F32)
        for cc in (0, 1):
            weights = jnp.exp(scores[cc] - top)
            weight_sum = weight_sum + jnp.sum(weights, axis=1, keepdims=True)
            values = kvall[cc, :, :, :, HD:2 * HD].reshape(1280, HD)
            mixed = mixed + jnp.dot(weights.astype(BF), values, preferred_element_type=F32)
        ao[i] = (mixed / weight_sum).astype(BF).reshape(2, 64, HD)

    att_here = None
    head_cols = pl.ds(pl.multiple_of(y * HD, HD), HD)
    att_dst = attin.at[mine_r, :, head_cols]
    for i in (3, 2, 1, 0):
        attend(i)
        src = (z - sg * i + NZ) % NZ
        if i > 0:
            put(ao.at[i, y], att_dst, R_ATT + y * 4 + mine_r, at_z(src))
        else:
            att_here = here(ao.at[0, y], att_dst)
        put(ao.at[i, oy], att_dst, R_ATT + y * 4 + mine_r, at_z(src, oy))
        if i == 3:
            wo_step(4)
        if i == 2:
            wo_onward(wo_y[:5])

    app_here = here(outg.at[s], app_ref.at[:, s % 16, :, :, head_cols_of])
    att_here.wait()
    for hh in (0, 1):
        for r in range(REQ):
            slot_ref = attin.at[r, :, pl.ds(hh * HD, HD)]
            mine = (r == mine_r) & (y == hh)

            @pl.when(jnp.logical_not(mine))
            def _():
                got(slot_ref, R_ATT + hh * 4 + r)
    wo_onward(wo_y[5:])
    for block, r in wo_sib:
        got(block, r)

    def partial_of(k):
        dest = (t + k) % 8
        left = attin[...].reshape(256, 512)

        for h in range(2):
            pbuf[k, :, pl.ds(h * 256, 256)] = jnp.dot(left, wog[dest * 2 + h], preferred_element_type=F32).astype(BF)
        return dest

    for k in range(1, 8):
        dest = partial_of(k)
        put(pbuf.at[k], rbuf.at[k], R_RS + k, s, dest)
    lax.fori_loop(17, 32, app_go, 0)
    partial_of(0)
    for k in range(1, 8):
        got(rbuf.at[k], R_RS + k)

    def total(i, carry):
        rows = pl.ds(pl.multiple_of(i * 32, 32), 32)
        value = pbuf[0, rows, :].astype(F32)
        for k in range(1, 8):
            value = value + rbuf[k, rows, :].astype(F32)
        out_ref[rows, :] = value.astype(BF)
        return carry
    lax.fori_loop(0, 8, total, 0)

    app_here.wait()

    def app_done(k, carry):
        o = (s + k) % 32
        cols = pl.ds(pl.multiple_of(o // 16 * HD, HD), HD)
        got(app_ref.at[:, o % 16, :, :, cols], R_APP + o)
        return carry
    lax.fori_loop(1, 32, app_done, 0)

    def app_sent(n, carry):
        send_app(n, False)
        return carry
    lax.fori_loop(0, 16, app_sent, 0)
    lax.fori_loop(17, 32, app_sent, 0)
    for copy in sends:
        copy.wait_send()


def body(hidden_in, ln_gain, ln_bias, w_qkv, w_out, cache_kv, cache_len, owner):
    width = w_qkv.shape[2]
    hid = hidden_in.reshape(256, hidden_in.shape[2])
    pair = np.arange(128) // 2
    freq = np.where(pair < ROT // 2, BASE_FREQ ** (-2.0 * pair / ROT), 0.0).astype(np.float32)[None]
    u = np.arange(1280)
    j, yy, zz = u % 80, (u // 80) % 2, u // 160
    key_new = np.where(j < 64, yy * 1024 + zz * 128 + j, FAR).astype(np.int32)[None]
    key_old = np.where(j < 64, FAR, yy * 256 + zz * 32 + j - 64).astype(np.int32)[None]
    orow = owner.reshape(1, 256)
    vmem = pl.BlockSpec(memory_space=pltpu.VMEM)
    anyw = pl.BlockSpec(memory_space=pl.ANY)
    attn, app = pl.pallas_call(
        kernel,
        out_shape=(jax.ShapeDtypeStruct((256, width), BF), jax.ShapeDtypeStruct((2, 16, SLOTS, 2, width), BF)),
        in_specs=[pl.BlockSpec(memory_space=pltpu.SMEM), anyw, vmem, vmem, anyw, anyw, anyw,
                  vmem, vmem, vmem, vmem],
        out_specs=(vmem, vmem),
        scratch_shapes=[
            pltpu.VMEM((2, 256, 4096), BF),
            pltpu.VMEM((2, 256, 4096), BF),
            pltpu.VMEM((2, NZ, 3, 256, 256), BF),
            pltpu.VMEM((2, 3, 256, 256), F32),
            pltpu.VMEM((2, REQ, 16, 2, HD), BF),
            pltpu.VMEM((2, 256, 128), F32),
            pltpu.VMEM((2, 256, 128), F32),
            pltpu.VMEM((REQ, 2, 64, HD), BF),
            pltpu.VMEM((REQ, 2, 80, 512), BF),
            pltpu.VMEM((4, 2, 64, HD), BF),
            pltpu.VMEM((2, NZ, 2, 80, 512), BF),
            pltpu.VMEM((REQ, 64, 512), BF),
            pltpu.VMEM((4, 2, 64, HD), BF),
            pltpu.VMEM((16, 512, 256), BF),
            pltpu.VMEM((8, 256, 512), BF),
            pltpu.VMEM((8, 256, 512), BF),
            pltpu.VMEM((32, 2, SLOTS, 2, HD), BF),
            pltpu.VMEM((2, 8, 256), jnp.int32),
            pltpu.SemaphoreType.DMA((N_SEND,)),
            pltpu.SemaphoreType.DMA((N_RECV,)),
            pltpu.SemaphoreType.DMA((16,)),
        ],
        compiler_params=pltpu.CompilerParams(
            collective_id=0, has_side_effects=True, vmem_limit_bytes=60 * 1024 * 1024),
    )(cache_len, hid, ln_gain.reshape(1, -1), ln_bias.reshape(1, -1), w_qkv, w_out, cache_kv,
      jnp.asarray(freq), jnp.asarray(key_new), jnp.asarray(key_old), orow)
    attn_out = attn.reshape(REQ, 64, width)
    appended = app.reshape(256, 2, width)
    return (attn_out, appended)


def solution(mesh):
    return jax.shard_map(
        body,
        mesh=mesh,
        in_specs=(
            P(None, "seq", None),
            P(),
            P(),
            P(None, "seq", "tp"),
            P("tp", "seq"),
            P(None, "seq", None, "tp"),
            P(),
            P("seq", None),
        ),
        out_specs=(P(None, "seq", "tp"), P("seq", None, "tp")),
        check_vma=False,
    )
```

```python
import jax
import jax.numpy as jnp
import numpy as np
from jax import lax
from jax.experimental import pallas as pl
from jax.experimental.pallas import tpu as pltpu
from jax.sharding import PartitionSpec as P

MESH = pl.DeviceIdType.MESH
HD = 256
ROT = 64
REQ = 4
SLOTS = 8
NZ = 8
EPSILON = 1e-05
BASE_FREQ = 10000.0
MASKED = -1e30
FAR = 1 << 20
BF = jnp.bfloat16
F32 = jnp.float32

R_WY, R_CACHE, R_TGT, R_HID = 0, 1, 2, 4
R_RING = 8
R_SIB = 22
R_Q = 38
R_KV = 46
R_FWD = 54
R_KVS = 62
R_ATT = 78
R_WOR = 86
R_WOY = 94
R_WOS = 103
R_RS = 121
R_APP = 129
N_RECV = 161
N_SEND = 192


def kernel(lens_ref, hid_ref, gain_ref, bias_ref, w_ref, wo_ref, cache_ref, freq_ref, kn_ref, kc_ref,
           orow_ref, out_ref, app_ref,
           hido, nbuf, wbuf, acc, craw, cosb, sinb, qs, kvs, qbuf, kvall, attin, ao, wog, pbuf, rbuf, outg, tgt,
           ssem, rsem, lsem, meet):
    s = lax.axis_index("seq")
    t = lax.axis_index("tp")
    y = s // 16
    z = (s // 2) % NZ
    c = s % 2
    oy = 1 - y
    sg = 1 - 2 * (z % 2)
    across = y * 16 * -2 + s + 16
    sib = s + 1 - 2 * c
    t1 = t + 1 - 2 * (t % 2)

    def at_z(zz, yy=None):
        return (y if yy is None else yy) * 16 + zz * 2 + c

    zp = (z + 1) % NZ
    zm = (z + NZ - 1) % NZ
    zpair = z + sg

    barrier = pltpu.get_barrier_semaphore()
    tps = ((t + 2) % 8, (t + 6) % 8)
    near = [(at_z(zp), t), (at_z(zm), t), (sib, t), (across, t), (across, t1)] + [(s, tt) for tt in tps]
    for ss, tt in near:
        pl.semaphore_signal(barrier, inc=1, device_id={"seq": ss, "tp": tt}, device_id_type=MESH)
    pl.semaphore_wait(barrier, 7)

    def meet_signal(n):
        for ss, tt in [(s, tt) for tt in tps] + ([(across, t1)] if n == 0 else []):
            pl.semaphore_signal(meet.at[n], inc=1, device_id={"seq": ss, "tp": tt}, device_id_type=MESH)

    def meet_wait(n):
        pl.semaphore_wait(meet.at[n], 3 if n == 0 else 2)

    sends = []
    locals_ = []

    def put(src, dst, r, seq, tp=None):
        copy = pltpu.make_async_remote_copy(
            src_ref=src, dst_ref=dst, send_sem=ssem.at[len(sends)], recv_sem=rsem.at[r],
            device_id={"seq": seq, "tp": t if tp is None else tp}, device_id_type=MESH)
        copy.start()
        sends.append(copy)

    def got(dst, r):
        pltpu.make_async_copy(dst, dst, rsem.at[r]).wait()

    def here(src, dst):
        copy = pltpu.make_async_copy(src, dst, lsem.at[len(locals_)])
        copy.start()
        locals_.append(copy)
        return copy

    rows_c = pl.ds(pl.multiple_of(c * 128, 128), 128)

    def wblock(yy, zz):
        return wbuf.at[yy, zz, :, rows_c, :]

    own_cols = pl.ds(pl.multiple_of(y * HD, HD), HD)
    oth_cols = pl.ds(pl.multiple_of(oy * HD, HD), HD)
    put(w_ref.at[:, :, oth_cols], wblock(y, z), R_WY, across)
    w_here = here(w_ref.at[:, :, own_cols], wblock(y, z))
    hid_here = here(hid_ref, hido.at[y])
    hid_rows = ((0, 64, t), (64, 64, t1), (128, 48, t), (176, 80, t1))
    for n, (first, count, via) in enumerate(hid_rows):
        put(hid_ref.at[pl.ds(first, count)], hido.at[y, pl.ds(first, count)], R_HID + n, across, via)
    put(cache_ref.at[:, :, :, oth_cols], craw.at[y], R_CACHE, across)
    cache_here = here(cache_ref.at[:, :, :, own_cols], craw.at[y])
    wo_cols = pl.ds(pl.multiple_of(c * 128, 128), 128)
    wo_here = here(wo_ref, wog.at[y * NZ + z, :, wo_cols])

    def spread_block(yy, zz, ring, ring_sem, sib_sem):
        block = wblock(yy, zz)
        for target, r in zip(ring, ring_sem):
            put(block, block, r, at_z(target))
        put(block, block, sib_sem, sib)

    meet_signal(0)
    w_here.wait()
    spread_block(y, z, (zp, zm), (R_RING, R_RING + 7), R_SIB)

    def layer_norm(yy, first=0, count=256):
        def step(i, carry):
            rows = pl.ds(pl.multiple_of(i * 16, 16), 16)
            wide = hido[yy, rows, :].astype(F32)
            center = jnp.mean(wide, axis=-1, keepdims=True)
            spread = wide - center
            variance = jnp.mean(spread * spread, axis=-1, keepdims=True)
            nbuf[yy, rows, :] = (spread * lax.rsqrt(variance + EPSILON) * gain_ref[...] + bias_ref[...]).astype(BF)
            return carry
        lax.fori_loop(first // 16, (first + count) // 16, step, 0)

    acc[...] = jnp.zeros_like(acc)

    def tables():
        spot = lax.broadcasted_iota(jnp.int32, (64, 128), 0)
        odd = lax.broadcasted_iota(jnp.int32, (64, 128), 1) % 2
        for yy in (0, 1):
            for r in range(REQ):
                position = spot + (lens_ref[r] + yy * 1024 + z * 128 + c * 64)
                angle = position.astype(F32) * freq_ref[...]
                cosb[yy, pl.ds(r * 64, 64), :] = jnp.cos(angle)
                turned = jnp.sin(angle)
                sinb[yy, pl.ds(r * 64, 64), :] = jnp.where(odd == 1, turned, -turned)
        before = lax.broadcasted_iota(jnp.int32, (256, 256), 0) < lax.broadcasted_iota(jnp.int32, (256, 256), 1)
        across_lanes = jnp.broadcast_to(orow_ref[...].astype(F32), (256, 256))
        same = jnp.where(before & (jnp.transpose(across_lanes) == across_lanes), 1, 0)
        slot = jnp.sum(same, axis=0, keepdims=True)
        tgt[y] = jnp.broadcast_to(orow_ref[...] * 16 + y * 8 + slot, (8, 256))

    got(wblock(oy, z), R_WY)
    spread_block(oy, z, (zp, zm), (R_RING + 1, R_RING + 8), R_SIB + 1)
    hid_here.wait()
    layer_norm(y, 0, 128)

    def project(tok_y, yy, zz, first=0, count=256):
        offset = pl.multiple_of(yy * 2048 + zz * 256, 256)
        rows = pl.ds(first, count)
        left = nbuf[tok_y, rows, pl.ds(offset, 256)]

        for i in range(3):
            acc[tok_y, i, rows, :] += jnp.dot(left, wbuf[yy, zz, i], preferred_element_type=F32)

    def ring_block(side, k):
        if k < 6:
            d, yy = k // 2 + 1, (y if k % 2 == 0 else oy)
        else:
            d, yy = 4, (y if side == 0 else oy)
        return yy, ((z + NZ - d) % NZ if side == 0 else (z + d) % NZ)

    def sib_wait(yy, zz, r):
        theirs = wbuf.at[yy, zz, :, pl.ds(pl.multiple_of((1 - c) * 128, 128), 128), :]
        got(theirs, r)

    waiting = [(y, z, R_SIB), (oy, z, R_SIB + 1)]
    for k in range(7):
        arrived = []
        for side in (0, 1):
            yy, zz = ring_block(side, k)
            got(wblock(yy, zz), R_RING + side * 7 + k)
            onward = None
            if k < 4:
                onward = k + 2
            elif (k == 4 and side == 0) or (k == 5 and side == 1):
                onward = 6
            ring = () if onward is None else ((zp if side == 0 else zm),)
            ring_sem = () if onward is None else (R_RING + side * 7 + onward,)
            r = R_SIB + 2 + side * 7 + k
            spread_block(yy, zz, ring, ring_sem, r)
            arrived.append((yy, zz, r))
        if k == 0:
            layer_norm(y, 128, 128)
        for yy, zz, r in waiting:
            sib_wait(yy, zz, r)
            project(y, yy, zz)
        waiting = arrived
        if k == 0:
            tables()
            put(tgt.at[y], tgt.at[y], R_TGT, across)
        if k in (1, 2, 3):
            meet_wait(k - 1)
            if k < 3:
                meet_signal(k)
        if k == 2:
            got(craw.at[oy], R_CACHE)
            cache_here.wait()
            for yy in (0, 1):
                raw = craw[yy]
                kvs[:, yy, 64:80, 0:HD] = raw[:, :, 0, :]
                kvs[:, yy, 64:80, HD:2 * HD] = raw[:, :, 1, :]
        if k == 3 or k == 5:
            n = k - 3
            if k == 5:
                wo_here.wait()
                mine = wog.at[y * NZ + z, :, wo_cols]
                put(mine, mine, R_WOR, at_z(zp))
                put(mine, mine, R_WOR + 4, at_z(zm))
                put(mine, mine, R_WOY, across)
                put(mine, mine, R_WOS, sib)
            for part in (n, n + 1):
                first, count, _ = hid_rows[part]
                got(hido.at[oy, pl.ds(first, count)], R_HID + part)
            layer_norm(oy, n * 64, 128)
        if k == 4 or k == 5:
            half = (k - 4) * 128

            def catch_up(n, carry):
                project(oy, n % 2, (z + NZ - 2 + n // 2) % NZ, half, 128)
                return carry
            lax.fori_loop(0, 10, catch_up, 0)
        if k == 5:
            for d in (3, NZ - 3):
                project(oy, y, (z + d) % NZ)
    for yy, zz, r in waiting:
        sib_wait(yy, zz, r)
        project(y, yy, zz)

    lane = lax.broadcasted_iota(jnp.int32, (64, 128), 1)
    even = lane % 2 == 0

    def finish(tok_y):
        def step(r, carry):
            rows = pl.ds(pl.multiple_of(r * 64, 64), 64)
            cosine = cosb[tok_y, rows, :]
            sine = sinb[tok_y, rows, :]

            def turn(i):
                head = acc[tok_y, i, rows, :]
                first = head[:, :128]
                swapped = jnp.where(even, pltpu.roll(first, 127, 1), pltpu.roll(first, 1, 1))
                return jnp.concatenate([first * cosine + swapped * sine, head[:, 128:]], axis=1).astype(BF)

            qs[r, tok_y] = turn(0)
            kvs[r, tok_y, pl.ds(0, 64), pl.ds(0, HD)] = turn(1)
            kvs[r, tok_y, pl.ds(0, 64), pl.ds(HD, HD)] = acc[tok_y, 2, rows, :].astype(BF)
            return carry
        lax.fori_loop(0, REQ, step, 0)

    def send_round(h, yy):
        held = []
        hops = ((3, (z - 3 * sg + NZ) % NZ), (2, (z + 2 * sg + NZ) % NZ), (1, (z - sg + NZ) % NZ))
        for i, dest in hops:
            put(kvs.at[dest // 2, yy], kvall.at[c, z, yy], R_KV + h * 4 + i, at_z(dest))
        for i, dest in hops:
            put(qs.at[dest // 2, yy], qbuf.at[i, yy], R_Q + h * 4 + i, at_z(dest))
        held.append(here(kvs.at[z // 2, yy], kvall.at[c, z, yy]))
        held.append(here(qs.at[z // 2, yy], qbuf.at[0, yy]))
        return held

    def forward_round(h, yy, held):
        held[0].wait()
        for i in range(4):
            block = kvall.at[c, (z - sg * i + NZ) % NZ, yy]
            if i > 0:
                got(block, R_KV + h * 4 + i)
            put(block, block, R_FWD + h * 4 + i, at_z(zpair))
            put(block, block, R_KVS + h * 8 + i, sib)

    def sibling_round(h, yy):
        for i in range(4):
            block = kvall.at[c, (zpair + sg * i + NZ) % NZ, yy]
            got(block, R_FWD + h * 4 + i)
            put(block, block, R_KVS + h * 8 + 4 + i, sib)

    finish(y)
    held_own = send_round(0, y)
    for yy, zz in ((oy, (z + NZ - 3) % NZ), (oy, (z + 3) % NZ)):
        project(oy, yy, zz)
    for yy, zz, r in waiting:
        project(oy, yy, zz)
    finish(oy)
    held_oth = send_round(1, oy)

    def wo_slot(yy, zz, rows=None):
        return wog.at[yy * NZ + zz, (pl.ds(0, 512) if rows is None else rows), wo_cols]

    def wo_sib_slot(yy, zz, rows=None):
        cols = pl.ds(pl.multiple_of((1 - c) * 128, 128), 128)
        return wog.at[yy * NZ + zz, (pl.ds(0, 512) if rows is None else rows), cols]

    wo_sib = [(wo_sib_slot(y, z), R_WOS)]
    wo_y = [(z, None, R_WOY)]

    def wo_step(d):
        for side in (0, 1):
            zz = (z + NZ - d) % NZ if side == 0 else (z + d) % NZ
            rows = None if d < 4 else pl.ds(side * 256, 256)
            block = wo_slot(y, zz, rows)
            got(block, R_WOR + side * 4 + d - 1)
            if d < 4:
                nxt = block if d < 3 else wo_slot(y, zz, pl.ds(side * 256, 256))
                put(nxt, nxt, R_WOR + side * 4 + d, at_z(zp if side == 0 else zm))
            n = 1 + (d - 1) * 2 + side
            put(block, block, R_WOY + n, across)
            put(block, block, R_WOS + n, sib)
            wo_sib.append((wo_sib_slot(y, zz, rows), R_WOS + n))
            wo_y.append((zz, rows, R_WOY + n))

    wo_step(1)
    forward_round(0, y, held_own)

    got(tgt.at[oy], R_TGT)
    row_id = lax.broadcasted_iota(jnp.int32, (256, 256), 0)

    def place(n, carry):
        total = jnp.zeros((256, HD), F32)
        for yy in (0, 1):
            for kv in (0, 1):
                mark = jnp.where(row_id + n * 256 == tgt[yy, 0:1, :] * 2 + kv, 1.0, 0.0).astype(BF)
                fresh = kvs[:, yy, 0:64, kv * HD:(kv + 1) * HD].reshape(256, HD)
                total = total + jnp.dot(mark, fresh, preferred_element_type=F32)
        outg[pl.ds(n * 8, 8)] = total.reshape(8, 2, SLOTS, 2, HD).astype(BF)
        return carry
    lax.fori_loop(0, 4, place, 0)

    sibling_round(0, y)
    forward_round(1, oy, held_oth)
    wo_step(2)
    sibling_round(1, oy)
    wo_step(3)

    def wo_onward(which):
        for zz, rows, r in which:
            block = wo_slot(oy, zz, rows)
            got(block, r)
            n = r - R_WOY
            put(block, block, R_WOS + 9 + n, sib)
            wo_sib.append((wo_sib_slot(oy, zz, rows), R_WOS + 9 + n))

    for h, yy in ((0, y), (1, oy)):
        for i in range(4):
            got(kvall.at[1 - c, (z - sg * i + NZ) % NZ, yy], R_KVS + h * 8 + i)
            got(kvall.at[1 - c, (zpair + sg * i + NZ) % NZ, yy], R_KVS + h * 8 + 4 + i)
            if i > 0:
                got(qbuf.at[i, yy], R_Q + h * 4 + i)
    held_own[1].wait()
    held_oth[1].wait()

    head_cols_of = pl.ds(pl.multiple_of(y * HD, HD), HD)

    def send_app(n, start):
        dest = jnp.where(n < 16, oy, y) * 16 + (s + n) % 16
        copy = pltpu.make_async_remote_copy(
            src_ref=outg.at[dest], dst_ref=app_ref.at[:, s % 16, :, :, head_cols_of],
            send_sem=ssem.at[N_SEND - 32 + n], recv_sem=rsem.at[R_APP + s],
            device_id={"seq": dest, "tp": t}, device_id_type=MESH)
        if start:
            copy.start()
        else:
            copy.wait_send()

    def app_go(n, carry):
        send_app(n, True)
        return carry
    lax.fori_loop(0, 16, app_go, 0)

    mine_r = z // 2
    length = lens_ref[mine_r]
    row = lax.broadcasted_iota(jnp.int32, (128, 1), 0)

    def attend(i):
        src = (z - sg * i + NZ) % NZ
        query = qbuf[i].reshape(128, HD)
        position = (row // 64) * 1024 + src * 128 + c * 64 + row % 64
        scores = []
        for cc in (0, 1):
            keys = kvall[cc, :, :, :, 0:HD].reshape(1280, HD)
            allowed = (kn_ref[...] + cc * 64 <= position) | (kc_ref[...] + cc * 16 < length)
            score = lax.dot_general(query, keys, (((1,), (1,)), ((), ())), preferred_element_type=F32)
            scores.append(jnp.where(allowed, score * (1.0 / 16.0), MASKED))
        top = jnp.maximum(jnp.max(scores[0], axis=1, keepdims=True), jnp.max(scores[1], axis=1, keepdims=True))
        weight_sum = jnp.zeros((128, 1), F32)
        mixed = jnp.zeros((128, HD), F32)
        for cc in (0, 1):
            weights = jnp.exp(scores[cc] - top)
            weight_sum = weight_sum + jnp.sum(weights, axis=1, keepdims=True)
            values = kvall[cc, :, :, :, HD:2 * HD].reshape(1280, HD)
            mixed = mixed + jnp.dot(weights.astype(BF), values, preferred_element_type=F32)
        ao[i] = (mixed / weight_sum).astype(BF).reshape(2, 64, HD)

    att_here = None
    head_cols = pl.ds(pl.multiple_of(y * HD, HD), HD)
    att_dst = attin.at[mine_r, :, head_cols]
    for i in (3, 2, 1, 0):
        attend(i)
        src = (z - sg * i + NZ) % NZ
        if i > 0:
            put(ao.at[i, y], att_dst, R_ATT + y * 4 + mine_r, at_z(src))
        else:
            att_here = here(ao.at[0, y], att_dst)
        put(ao.at[i, oy], att_dst, R_ATT + y * 4 + mine_r, at_z(src, oy))
        if i == 3:
            wo_step(4)
        if i == 2:
            wo_onward(wo_y[:5])

    app_here = here(outg.at[s], app_ref.at[:, s % 16, :, :, head_cols_of])
    att_here.wait()
    for hh in (0, 1):
        for r in range(REQ):
            slot_ref = attin.at[r, :, pl.ds(hh * HD, HD)]
            mine = (r == mine_r) & (y == hh)

            @pl.when(jnp.logical_not(mine))
            def _():
                got(slot_ref, R_ATT + hh * 4 + r)
    wo_onward(wo_y[5:])
    for block, r in wo_sib:
        got(block, r)

    def partial_of(k):
        dest = (t + k) % 8
        left = attin[...].reshape(256, 512)

        for h in range(2):
            pbuf[k, :, pl.ds(h * 256, 256)] = jnp.dot(left, wog[dest * 2 + h], preferred_element_type=F32).astype(BF)
        return dest

    for k in (4, 5, 3, 2, 6, 7, 1):
        dest = partial_of(k)
        put(pbuf.at[k], rbuf.at[k], R_RS + k, s, dest)
    lax.fori_loop(17, 32, app_go, 0)
    partial_of(0)
    for k in range(1, 8):
        got(rbuf.at[k], R_RS + k)

    def total(i, carry):
        rows = pl.ds(pl.multiple_of(i * 32, 32), 32)
        value = pbuf[0, rows, :].astype(F32)
        for k in range(1, 8):
            value = value + rbuf[k, rows, :].astype(F32)
        out_ref[rows, :] = value.astype(BF)
        return carry
    lax.fori_loop(0, 8, total, 0)

    app_here.wait()

    def app_done(k, carry):
        o = (s + k) % 32
        cols = pl.ds(pl.multiple_of(o // 16 * HD, HD), HD)
        got(app_ref.at[:, o % 16, :, :, cols], R_APP + o)
        return carry
    lax.fori_loop(1, 32, app_done, 0)

    def app_sent(n, carry):
        send_app(n, False)
        return carry
    lax.fori_loop(0, 16, app_sent, 0)
    lax.fori_loop(17, 32, app_sent, 0)
    for copy in sends:
        copy.wait_send()


def body(hidden_in, ln_gain, ln_bias, w_qkv, w_out, cache_kv, cache_len, owner):
    width = w_qkv.shape[2]
    hid = hidden_in.reshape(256, hidden_in.shape[2])
    pair = np.arange(128) // 2
    freq = np.where(pair < ROT // 2, BASE_FREQ ** (-2.0 * pair / ROT), 0.0).astype(np.float32)[None]
    u = np.arange(1280)
    j, yy, zz = u % 80, (u // 80) % 2, u // 160
    key_new = np.where(j < 64, yy * 1024 + zz * 128 + j, FAR).astype(np.int32)[None]
    key_old = np.where(j < 64, FAR, yy * 256 + zz * 32 + j - 64).astype(np.int32)[None]
    orow = owner.reshape(1, 256)
    vmem = pl.BlockSpec(memory_space=pltpu.VMEM)
    anyw = pl.BlockSpec(memory_space=pl.ANY)
    attn, app = pl.pallas_call(
        kernel,
        out_shape=(jax.ShapeDtypeStruct((256, width), BF), jax.ShapeDtypeStruct((2, 16, SLOTS, 2, width), BF)),
        in_specs=[pl.BlockSpec(memory_space=pltpu.SMEM), anyw, vmem, vmem, anyw, anyw, anyw,
                  vmem, vmem, vmem, vmem],
        out_specs=(vmem, vmem),
        scratch_shapes=[
            pltpu.VMEM((2, 256, 4096), BF),
            pltpu.VMEM((2, 256, 4096), BF),
            pltpu.VMEM((2, NZ, 3, 256, 256), BF),
            pltpu.VMEM((2, 3, 256, 256), F32),
            pltpu.VMEM((2, REQ, 16, 2, HD), BF),
            pltpu.VMEM((2, 256, 128), F32),
            pltpu.VMEM((2, 256, 128), F32),
            pltpu.VMEM((REQ, 2, 64, HD), BF),
            pltpu.VMEM((REQ, 2, 80, 512), BF),
            pltpu.VMEM((4, 2, 64, HD), BF),
            pltpu.VMEM((2, NZ, 2, 80, 512), BF),
            pltpu.VMEM((REQ, 64, 512), BF),
            pltpu.VMEM((4, 2, 64, HD), BF),
            pltpu.VMEM((16, 512, 256), BF),
            pltpu.VMEM((8, 256, 512), BF),
            pltpu.VMEM((8, 256, 512), BF),
            pltpu.VMEM((32, 2, SLOTS, 2, HD), BF),
            pltpu.VMEM((2, 8, 256), jnp.int32),
            pltpu.SemaphoreType.DMA((N_SEND,)),
            pltpu.SemaphoreType.DMA((N_RECV,)),
            pltpu.SemaphoreType.DMA((16,)),
            pltpu.SemaphoreType.REGULAR((3,)),
        ],
        compiler_params=pltpu.CompilerParams(
            collective_id=0, has_side_effects=True, vmem_limit_bytes=60 * 1024 * 1024),
    )(cache_len, hid, ln_gain.reshape(1, -1), ln_bias.reshape(1, -1), w_qkv, w_out, cache_kv,
      jnp.asarray(freq), jnp.asarray(key_new), jnp.asarray(key_old), orow)
    attn_out = attn.reshape(REQ, 64, width)
    appended = app.reshape(256, 2, width)
    return (attn_out, appended)


def solution(mesh):
    return jax.shard_map(
        body,
        mesh=mesh,
        in_specs=(
            P(None, "seq", None),
            P(),
            P(),
            P(None, "seq", "tp"),
            P("tp", "seq"),
            P(None, "seq", None, "tp"),
            P(),
            P("seq", None),
        ),
        out_specs=(P(None, "seq", "tp"), P("seq", None, "tp")),
        check_vma=False,
    )
```
